32 devices in a mesh: dp: 4 (over y, x), sp: 8 (over z, core).
Axes of the slice: x: 2, y: 2, z: 4, core: 2. Of those that a mesh axis runs over, the one named last changes fastest.
Arguments:
- inputs: bfloat16 [3, 8, 8, 200, 768], P(None, 'dp', None, 'sp'), may hold values from -6 to 6
- cotangent: bfloat16 [3, 8, 8, 200, 768], P(None, 'dp', None, 'sp'), may hold values from -6 to 6
- params: bfloat16 [10043392], P(('dp', 'sp'))
- clip_counts: int32 [3, 4], P(None, 'dp'), may hold values from 1 to 2, as said below
- slot_live: int32 [3, 8, 200], P(None, 'dp', 'sp'), may hold values from 0 to 1, as said below
Outputs:
- layer_out: bfloat16 [3, 8, 8, 200, 768], P(None, 'dp', None, 'sp')
- input_grad: bfloat16 [3, 8, 8, 200, 768], P(None, 'dp', None, 'sp')
- param_grad: float32 [10043392], P(('dp', 'sp'))
The draws below stay inside these ranges and needn't reach their ends.
Inputs may be any that keep to these rules, and one draw needn't show every extreme that they name: `slot_live`: each clip slot has exactly 196 place slots with value 1. In each micro-batch, group g uses its clip slots 0 to clip_counts[m, g] - 1; some group of some micro-batch uses all 2.
All inputs are finite; a program needn't handle non-finite values.
Results may differ from the reference program's by a relative error of at most 0.018.
Values may be sent and summed in bfloat16 or wider, within the bound.
No kernel may reach another device: no remote copies, remote signals or barrier semaphores. Data moves between devices by JAX's collectives and lax.ppermute only.
A program may use at most 384 MiB of HBM per device.

```python
import math
import jax
import jax.numpy as jnp
from jax import lax

D = 768
H = 12
FF = 3072
F = 8
P_SIZE = 196
MB = 3
CG = 2
NC = 8
NP = 200
NPARAM = 10043392
N_DP = 4


def param_layout():
    return [((D,), 1.0, 0.1), ((D,), 0.0, 0.2), ((D, 3 * D), 0.0, D ** (-0.5)), ((D,), 0.0, 0.2), ((D,), 0.0, 0.2), ((D, D), 0.0, 2.5 * D ** (-0.5)), ((D,), 0.0, 0.2), ((D, D), 0.0, D ** (-0.5)), ((D,), 0.0, 0.2), ((D,), 1.0, 0.1), ((D,), 0.0, 0.2), ((D, 3 * D), 0.0, D ** (-0.5)), ((D,), 0.0, 0.2), ((D,), 0.0, 0.2), ((D, D), 0.0, 6.0 * D ** (-0.5)), ((D,), 0.0, 0.2), ((D,), 1.0, 0.1), ((D,), 0.0, 0.2), ((D, FF), 0.0, D ** (-0.5)), ((FF,), 0.0, 0.2), ((FF, D), 0.0, FF ** (-0.5)), ((D,), 0.0, 0.2)]


def draw_params(key, part):
    blocks = []
    filled = 0
    for number, (layout, center, spread) in enumerate(param_layout()):
        length = math.prod(layout)
        sub_key = jax.random.fold_in(key, number)
        noise = jax.random.normal(sub_key, (length,), jnp.float32)
        blocks.append(center + spread * noise)
        filled = filled + length
    blocks.append(0.02 * jax.random.normal(jax.random.fold_in(key, 99), (NPARAM - filled,), jnp.float32))
    return jnp.concatenate(blocks).astype(jnp.bfloat16)


def draw_clip_counts(key, part):
    entries = MB * N_DP
    lowest = max(1, CG // 2)
    drawn = jax.random.randint(jax.random.fold_in(key, 1), (entries,), lowest, CG + 1)
    full_at = jax.random.randint(jax.random.fold_in(key, 2), (), 0, entries)
    low_at = (full_at + 1 + jax.random.randint(jax.random.fold_in(key, 3), (), 0, entries - 1)) % entries
    drawn = drawn.at[full_at].set(CG).at[low_at].set(lowest)
    return drawn.reshape(MB, N_DP).astype(jnp.int32)


def one_order(base_key, index):
    return jax.random.permutation(jax.random.fold_in(base_key, index), NP)


def draw_slot_live(key, part):
    base_key = jax.random.fold_in(key, 7)
    indices = jnp.arange(MB * NC, dtype=jnp.int32)
    orders = jax.vmap(one_order, in_axes=(None, 0))(base_key, indices)
    return (orders < P_SIZE).astype(jnp.int32).reshape(MB, NC, NP)


def steps_of(own_key, extent, shards, least, top_value):
    def one(dim, shards_of):
        heights = jax.random.uniform(jax.random.fold_in(jax.random.fold_in(own_key, 6), dim), (shards_of,), jnp.float32, least / len(shards), top_value / len(shards))
        return jnp.repeat(jnp.exp(heights), extent[dim] // shards_of).reshape((-1,) + (1,) * (len(extent) - dim - 1))

    factor_of = one(*shards[0])
    for cut in shards[1:]:
        factor_of = factor_of * one(*cut)
    return factor_of


def normal_values(stream_key, shape, width, reach, shards=(), kind=jnp.bfloat16):
    loudness = steps_of(stream_key, shape, shards, -0.22, 0.18) if shards else 1.0
    values = jax.random.normal(stream_key, shape, jnp.float32) * width * loudness
    return jnp.minimum(jnp.maximum(values, -reach), reach).astype(kind)


def setup_inputs(seed: int = 0) -> dict:
    arg_keys = jax.random.split(jax.random.key(seed), 6)
    return {
        "inputs": normal_values(arg_keys[0], (MB, NC, F, NP, D), 1.0, 6.0, ((1, 4), (3, 8))),
        "cotangent": normal_values(arg_keys[1], (MB, NC, F, NP, D), 1.0, 6.0, ((1, 4), (3, 8))),
        "params": draw_params(jax.random.fold_in(arg_keys[5], 71), 0),
        "clip_counts": draw_clip_counts(jax.random.fold_in(arg_keys[5], 71), 0),
        "slot_live": draw_slot_live(jax.random.fold_in(arg_keys[5], 71), 0),
    }


@jax.custom_vjp
def low(v):
    return lax.optimization_barrier(v.astype(jnp.bfloat16)).astype(jnp.float32)

@jax.custom_vjp
def low_back(v):
    return v

def low_keep(v):
    return (low(v), None)

def low_pass(kept, grad):
    return (grad,)

def back_keep(v):
    return (v, None)

def back_low(kept, grad):
    return (low(grad),)
low.defvjp(low_keep, low_pass)
low_back.defvjp(back_keep, back_low)
EPS = 1e-06
MASKED = -1000000000.0
HIGHEST = lax.Precision.HIGHEST

def segment_shapes(model_width, hidden_width):
    return [(model_width,), (model_width,), (model_width, 3 * model_width), (model_width,), (model_width,), (model_width, model_width), (model_width,), (model_width, model_width), (model_width,), (model_width,), (model_width,), (model_width, 3 * model_width), (model_width,), (model_width,), (model_width, model_width), (model_width,), (model_width,), (model_width,), (model_width, hidden_width), (hidden_width,), (hidden_width, model_width), (model_width,)]

def unpack(flat_params, model_width, hidden_width):
    pieces = []
    offset = 0
    for layout in segment_shapes(model_width, hidden_width):
        length = math.prod(layout)
        pieces.append(flat_params[offset:offset + length].reshape(layout))
        offset = offset + length
    return pieces

def layer_norm(values, norm_gain, norm_shift):
    center = values - lax.optimization_barrier(jnp.mean(values, axis=-1, keepdims=True))
    spread = lax.optimization_barrier(jnp.mean(center * center, axis=-1, keepdims=True))
    return center * lax.rsqrt(spread + EPS) * norm_gain + norm_shift

def matmul(left_side, right_side):
    return jnp.dot(left_side, right_side, precision=HIGHEST)

def attention_block(normed, weight, query_bias, value_bias, key_live, head_count):
    bias_all = jnp.concatenate([query_bias, jnp.zeros_like(query_bias), value_bias])
    packed = low(low_back(matmul(normed, weight) + bias_all))
    model_width = normed.shape[-1]
    leading = normed.shape[:-1]
    head_size = model_width // head_count
    query_rows = packed[..., :model_width].reshape(leading + (head_count, head_size))
    key_rows = packed[..., model_width:2 * model_width].reshape(leading + (head_count, head_size))
    value_rows = packed[..., 2 * model_width:].reshape(leading + (head_count, head_size))
    scores = jnp.einsum('bqhd,bkhd->bhqk', query_rows, key_rows, precision=HIGHEST) * head_size ** (-0.5)
    if key_live is not None:
        scores = jnp.where(key_live[:, None, None, :], scores, MASKED)
    softmax_rows = low(jax.nn.softmax(low_back(scores), axis=-1))
    mixed_rows = jnp.einsum('bhqk,bkhd->bqhd', softmax_rows, value_rows, precision=HIGHEST)
    return low(low_back(mixed_rows.reshape(normed.shape)))

def clip_forward(clip_in, clip_live, pieces):
    time_gain, time_shift, time_qkv, time_q_bias, time_v_bias, time_out, time_out_bias, fc_weight, fc_bias, space_gain, space_shift, space_qkv, space_q_bias, space_v_bias, space_out, space_out_bias, mlp_gain, mlp_shift, up_weight, up_bias, down_weight, down_bias = pieces
    seq_time = jnp.swapaxes(clip_in, 0, 1)
    merged = attention_block(low(layer_norm(seq_time, time_gain, time_shift)), time_qkv, time_q_bias, time_v_bias, None, H)
    mixed_rows = low(low_back(matmul(merged, time_out) + time_out_bias))
    first_rows = seq_time + low_back(matmul(mixed_rows, fc_weight) + fc_bias)
    start_rows = low(low_back(jnp.swapaxes(first_rows, 0, 1)))
    key_live = jnp.broadcast_to(clip_live > 0.5, (clip_in.shape[0], clip_in.shape[1]))
    merged_space = attention_block(low(layer_norm(start_rows, space_gain, space_shift)), space_qkv, space_q_bias, space_v_bias, key_live, H)
    middle = start_rows + low_back(matmul(merged_space, space_out) + space_out_bias)
    normed_mlp = low(layer_norm(middle, mlp_gain, mlp_shift))
    upper = low_back(matmul(normed_mlp, up_weight) + up_bias)
    active = low(jax.nn.gelu(upper, approximate=False))
    result = middle + low_back(matmul(active, down_weight) + down_bias)
    return low(result) * clip_live[None, :, None]

def reference(inputs, cotangent, params, clip_counts, slot_live):
    flat_params = params.astype(jnp.float32)
    slot_rank = jnp.arange(NC, dtype=jnp.int32)
    in_use = slot_rank[None, :] % CG < jnp.repeat(clip_counts, CG, axis=1)
    live_mask = slot_live.astype(jnp.float32) * in_use[:, :, None].astype(jnp.float32)
    clips_in = inputs.reshape((MB * NC, F, NP, D))
    clips_cot = cotangent.reshape((MB * NC, F, NP, D))
    clips_live = live_mask.reshape((MB * NC, NP))

    def one_clip(running, item):
        clip_in, clip_cot, clip_live = item

        def forward(values, weights):
            return clip_forward(values, clip_live, unpack(weights, D, FF))
        result, pullback = jax.vjp(forward, clip_in.astype(jnp.float32), flat_params)
        grad_in, grad_flat = pullback(clip_cot.astype(jnp.float32))
        return (running + grad_flat, (result.astype(jnp.bfloat16), grad_in.astype(jnp.bfloat16)))
    running, (results, grads_in) = lax.scan(one_clip, jnp.zeros((NPARAM,), jnp.float32), (clips_in, clips_cot, clips_live))
    return (results.reshape(inputs.shape), grads_in.reshape(inputs.shape), running)
```

```python
import math

import jax
import jax.numpy as jnp
from jax import lax
from jax.experimental import pallas as pl
from jax.experimental.pallas import tpu as pltpu
from jax.sharding import PartitionSpec as P

H = 12
FF = 3072
EPS = 1e-06
MASKED = -1000000000.0
LANES = 128
BOTH = ("dp", "sp")
BF = jnp.bfloat16
F32 = jnp.float32


def segment_shapes(d, ff):
    return [
        (d,), (d,), (d, 3 * d), (d,), (d,), (d, d), (d,), (d, d), (d,),
        (d,), (d,), (d, 3 * d), (d,), (d,), (d, d), (d,),
        (d,), (d,), (d, ff), (ff,), (ff, d), (d,),
    ]


def pair_masks(rows):
    lane = lax.broadcasted_iota(jnp.int32, (rows, LANES), 1)
    return lane < LANES // 2


def dot_t(a, b):
    return lax.dot_general(a, b, (((1,), (1,)), ((), ())), preferred_element_type=F32)


def dot_l(a, b):
    return lax.dot_general(a, b, (((0,), (0,)), ((), ())), preferred_element_type=F32)


def dot(a, b):
    return jnp.dot(a, b, preferred_element_type=F32)


def softmax_of(q, k, keep):
    s = jnp.where(keep, dot_t(q, k), MASKED)
    top = jnp.max(s, axis=-1, keepdims=True)
    e = jnp.exp(s - top)
    return e * (1.0 / jnp.sum(e, axis=-1, keepdims=True))


def attend_kernel(q_ref, k_ref, v_ref, m_ref, o_ref):
    keep = m_ref[0] > 0.5
    rows, width = q_ref.shape[1], q_ref.shape[2]
    first = pair_masks(rows)
    for at in range(0, width, LANES):
        q = q_ref[0, :, at : at + LANES] * jnp.asarray(0.125, BF)
        k = k_ref[0, :, at : at + LANES]
        v = v_ref[0, :, at : at + LANES]
        zero = jnp.zeros_like(q)
        pa = softmax_of(jnp.where(first, q, zero), k, keep).astype(BF)
        pb = softmax_of(jnp.where(first, zero, q), k, keep).astype(BF)
        o_ref[0, :, at : at + LANES] = jnp.where(first, dot(pa, v), dot(pb, v)).astype(BF)


def attend_back_kernel(q_ref, k_ref, v_ref, m_ref, d_ref, dq_ref, dk_ref, dv_ref):
    keep = m_ref[0] > 0.5
    rows, width = q_ref.shape[1], q_ref.shape[2]
    first = pair_masks(rows)
    for at in range(0, width, LANES):
        q = q_ref[0, :, at : at + LANES] * jnp.asarray(0.125, BF)
        k = k_ref[0, :, at : at + LANES]
        v = v_ref[0, :, at : at + LANES]
        d = d_ref[0, :, at : at + LANES]
        zero = jnp.zeros_like(q)
        parts = []
        for here in (True, False):
            pick = (lambda t: jnp.where(first, t, zero)) if here else (lambda t: jnp.where(first, zero, t))
            p = softmax_of(pick(q), k, keep)
            dp = dot_t(pick(d), v)
            ds = (p * (dp - jnp.sum(p * dp, axis=-1, keepdims=True))).astype(BF)
            parts.append((dot(ds, k) * 0.125, dot_l(ds, q), dot_l(p.astype(BF), d)))
        for ref, a, b in zip((dq_ref, dk_ref, dv_ref), *parts):
            ref[0, :, at : at + LANES] = jnp.where(first, a, b).astype(BF)


def head_split(width):
    for parts in (2, 3, 1):
        if width % (parts * LANES) == 0:
            return parts
    return 1


def attention_specs(packed, keep, d):
    parts = head_split(d)
    w = d // parts
    rows = packed.shape[1]
    own = lambda third: pl.BlockSpec((1, rows, w), lambda i, j: (i, 0, third * parts + j))
    one = keep.shape[0] == 1
    mask = pl.BlockSpec((1,) + keep.shape[1:], lambda i, j: (0 if one else i, 0, 0))
    flat = pl.BlockSpec((1, rows, w), lambda i, j: (i, 0, j))
    return parts, own, mask, flat


def attend(packed, keep, d):
    n, rows, _ = packed.shape
    parts, own, mask, flat = attention_specs(packed, keep, d)
    return pl.pallas_call(
        attend_kernel,
        grid=(n, parts),
        in_specs=[own(0), own(1), own(2), mask],
        out_specs=flat,
        out_shape=jax.ShapeDtypeStruct((n, rows, d), BF),
        cost_estimate=pl.CostEstimate(
            flops=4 * n * rows * rows * d * 2,
            bytes_accessed=n * rows * d * 8,
            transcendentals=n * rows * rows * (d // 64),
        ),
        name="attend",
    )(packed, packed, packed, keep)


def attend_back(packed, keep, grad, d):
    n, rows, _ = packed.shape
    parts, own, mask, flat = attention_specs(packed, keep, d)
    shape = jax.ShapeDtypeStruct((n, rows, d), BF)
    return pl.pallas_call(
        attend_back_kernel,
        grid=(n, parts),
        in_specs=[own(0), own(1), own(2), mask, flat],
        out_specs=[flat, flat, flat],
        out_shape=[shape, shape, shape],
        cost_estimate=pl.CostEstimate(
            flops=10 * n * rows * rows * d * 2,
            bytes_accessed=n * rows * d * 14,
            transcendentals=n * rows * rows * (d // 64),
        ),
        name="attend_back",
    )(packed, packed, packed, keep, grad)


def flip_perm(dp_bits=0, sp_bits=0):
    return [(d * 8 + s, (d ^ dp_bits) * 8 + (s ^ sp_bits)) for d in range(4) for s in range(8)]


def send(value, dp_bits=0, sp_bits=0):
    return lax.ppermute(value, BOTH, flip_perm(dp_bits, sp_bits))


def pick(stack, at):
    return lax.dynamic_index_in_dim(stack, at, 0, keepdims=False)


def place_of():
    dp, sp = lax.axis_index("dp"), lax.axis_index("sp")
    return jnp.stack([dp, sp >> 1, sp & 1]).astype(jnp.int32)


def round_up(value, step):
    return -(-value // step) * step


class Plan:
    def __init__(self, rows):
        self.rows = rows
        self.part = round_up(-(-rows // 4), 16)
        self.gap = 4 * self.part - rows
        self.block = 32 * self.part

    def padded(self, row):
        return row + self.gap * (row // self.rows)


def assemble_kernel(pos_ref, *refs):
    ins, out, buf, sem_in, sem_out = refs[:8], refs[8], refs[9], refs[10], refs[11]
    dp, z, core = pos_ref[0], pos_ref[1], pos_ref[2]
    loads = []
    for j in range(8):
        for k in range(4):
            at = j * 4 + k
            load = pltpu.make_async_copy(ins[j].at[k], buf.at[at], sem_in.at[at])
            load.start()
            loads.append(load)
    stores = []
    for j in range(8):
        for k in range(4):
            at = j * 4 + k
            loads[at].wait()
            to = ((z ^ k) * 2 + (core ^ (j // 4))) * 4 + (dp ^ (j % 4))
            store = pltpu.make_async_copy(buf.at[at], out.at[to], sem_out.at[at])
            store.start()
            stores.append(store)
    for store in stores:
        store.wait()


def assemble(pos, pieces):
    part = pieces[0].shape[1]
    any_spec = pl.BlockSpec(memory_space=pl.ANY)
    out = pl.pallas_call(
        assemble_kernel,
        grid_spec=pltpu.PrefetchScalarGridSpec(
            num_scalar_prefetch=1,
            grid=(1,),
            in_specs=[any_spec] * 8,
            out_specs=any_spec,
            scratch_shapes=[
                pltpu.VMEM((32, part, LANES), BF),
                pltpu.SemaphoreType.DMA((32,)),
                pltpu.SemaphoreType.DMA((32,)),
            ],
        ),
        out_shape=jax.ShapeDtypeStruct((32, part, LANES), BF),
        cost_estimate=pl.CostEstimate(flops=0, bytes_accessed=32 * part * LANES * 4, transcendentals=0),
        name="assemble",
    )(pos, *pieces)
    return out.reshape(32 * part, LANES)


def gather_blocks(shard, plan, pos):
    dp = pos[0]
    mine = jnp.pad(shard.reshape(plan.rows, LANES), ((0, plan.gap), (0, 0)))
    mine = mine.reshape(4, plan.part, LANES)
    spread = jnp.zeros_like(mine)
    for k in range(4):
        piece = pick(mine, dp ^ k)
        got = piece if k == 0 else send(piece, k)
        spread = lax.dynamic_update_slice(spread, got[None], (dp ^ k, 0, 0))
    blocks = []
    for b in range(4):
        piece = spread[b]
        line = jnp.stack([piece] + [send(piece, 0, 2 * k) for k in range(1, 4)])
        own = [line] + [send(line, k) for k in range(1, 4)]
        other = [send(part, 0, 1) for part in own]
        blocks.append(assemble(pos, own + other))
    return blocks


CHUNK = 1152


def unflatten(src, base, off, rows, width, plan):
    lanes = width // LANES
    step_rows = CHUNK // lanes
    size = src.shape[0]
    window = round_up(CHUNK + plan.gap + 16, 16)

    def where_from(i):
        first = off + CHUNK * i
        at = first + plan.gap * (first // plan.rows) - base
        return first, at, jnp.minimum(at // 16 * 16, size - window)

    def kernel(in_ref, out_ref, wide):
        first, at, start = where_from(pl.program_id(0))
        delta = at - start
        left = plan.rows - first % plan.rows
        wide[...] = in_ref[...].astype(F32)

        @pl.when(left >= CHUNK)
        def _():
            for b in range(lanes):
                got = wide[pl.ds(delta + b, step_rows, stride=lanes), :]
                out_ref[:, b * LANES : (b + 1) * LANES] = got.astype(BF)

        @pl.when(left < CHUNK)
        def _():
            row = lax.broadcasted_iota(jnp.int32, (step_rows, LANES), 0) * lanes
            for b in range(lanes):
                near = wide[pl.ds(delta + b, step_rows, stride=lanes), :]
                far = wide[pl.ds(delta + b + plan.gap, step_rows, stride=lanes), :]
                got = jnp.where(row + b < left, near, far)
                out_ref[:, b * LANES : (b + 1) * LANES] = got.astype(BF)

    return pl.pallas_call(
        kernel,
        grid=(rows // step_rows,),
        in_specs=[
            pl.BlockSpec(
                (pl.Element(window), pl.Element(LANES)),
                lambda i: (pl.multiple_of(where_from(i)[2], 16), 0),
            )
        ],
        out_specs=pl.BlockSpec((step_rows, width), lambda i: (i, 0)),
        out_shape=jax.ShapeDtypeStruct((rows, width), BF),
        scratch_shapes=[pltpu.VMEM((window, LANES), F32)],
        cost_estimate=pl.CostEstimate(flops=0, bytes_accessed=rows * width * 4, transcendentals=0),
        name="unflatten",
    )(src)


def flatten(pos, b, mats, vecs, plan):
    part = plan.part
    shapes = []
    for off, mat in mats:
        lanes = mat.shape[1] // LANES
        shapes.append((off, mat.shape[0], lanes, round_up(-(-part // lanes) + 8, 8)))
    pad = round_up(max([w * c for _, _, c, w in shapes] + [v.shape[0] for _, v in vecs]), 8) + 8

    def first_row(t, pos_ref):
        z = pos_ref[1] ^ (t % 4)
        core = jnp.where(t < 16, 1 - pos_ref[2], pos_ref[2])
        quarter = pos_ref[0] ^ (t // 4 % 4)
        return (8 * b + z * 2 + core) * plan.rows + quarter * part

    def start_row(p0, off, rows, lanes, w):
        return jnp.minimum(jnp.maximum(p0 - off, 0) // lanes // 8 * 8, rows - w)

    def kernel(pos_ref, *refs):
        ins = refs[: len(mats)]
        vins = refs[len(mats) : len(mats) + len(vecs)]
        theirs, ours, wide = refs[len(mats) + len(vecs) :]
        t = pl.program_id(0)
        p0 = first_row(t, pos_ref)
        for (off, rows, lanes, w), ref in zip(shapes, ins):

            @pl.when((p0 + part > off) & (p0 < off + rows * lanes))
            def _():
                at = off + lanes * start_row(p0, off, rows, lanes, w) - p0 + pad
                for c in range(lanes):
                    wide[pl.ds(at + c, w, stride=lanes), :] = ref[:, c * LANES : (c + 1) * LANES]

        for (off, vec), ref in zip(vecs, vins):
            n = vec.shape[0]

            @pl.when((p0 + part > off) & (p0 < off + n))
            def _():
                at = off - p0 + pad
                for r in range(n):
                    wide[pl.ds(at + r, 1), :] = ref[r : r + 1, :]

        got = wide[pad : pad + part, :].astype(BF)

        @pl.when(t < 16)
        def _():
            theirs[0] = got

        @pl.when(t >= 16)
        def _():
            ours[0] = got

    in_specs = [
        pl.BlockSpec(
            (pl.Element(w), pl.Element(lanes * LANES)),
            lambda t, p, off=off, rows=rows, lanes=lanes, w=w: (
                pl.multiple_of(start_row(first_row(t, p), off, rows, lanes, w), 8),
                0,
            ),
        )
        for off, rows, lanes, w in shapes
    ] + [pl.BlockSpec(v.shape, lambda t, p: (0, 0)) for _, v in vecs]
    shape = jax.ShapeDtypeStruct((16, part, LANES), BF)
    theirs, ours = pl.pallas_call(
        kernel,
        grid_spec=pltpu.PrefetchScalarGridSpec(
            num_scalar_prefetch=1,
            grid=(32,),
            in_specs=in_specs,
            out_specs=[
                pl.BlockSpec((1, part, LANES), lambda t, p: (jnp.minimum(t, 15), 0, 0)),
                pl.BlockSpec((1, part, LANES), lambda t, p: (jnp.maximum(t - 16, 0), 0, 0)),
            ],
            scratch_shapes=[pltpu.VMEM((2 * pad + part, LANES), F32)],
        ),
        out_shape=[shape, shape],
        cost_estimate=pl.CostEstimate(flops=0, bytes_accessed=plan.block * LANES * 6, transcendentals=0),
        name="flatten",
    )(pos, *[m for _, m in mats], *[v for _, v in vecs])
    return theirs.reshape(4, 4, part, LANES), ours.reshape(4, 4, part, LANES)


def reduce_block(theirs, ours):
    ours = (ours.astype(F32) + send(theirs, 0, 1).astype(F32)).astype(BF)
    total = ours[0].astype(F32)
    for k in range(1, 4):
        total = total + send(ours[k], k).astype(F32)
    line = total.astype(BF)
    total = line[0].astype(F32)
    for k in range(1, 4):
        total = total + send(line[k], 0, 2 * k).astype(F32)
    return total


def return_quarters(quarters, plan, pos):
    stack = jnp.stack(quarters)
    dp = pos[0]
    out = jnp.zeros_like(stack)
    for k in range(4):
        piece = pick(stack, dp ^ k)
        got = piece if k == 0 else send(piece, k)
        out = lax.dynamic_update_slice(out, got[None], (dp ^ k, 0, 0))
    return out.reshape(4 * plan.part, LANES)[: plan.rows].reshape(-1)


def segment_rows(d, ff):
    spans, at = [], 0
    for shape in segment_shapes(d, ff):
        length = math.prod(shape)
        spans.append((at, at + length, shape))
        at += length
    return spans, at


def cut(blocks, lo, hi):
    size = blocks[0].shape[0]
    pieces = []
    for i, block in enumerate(blocks):
        a, b = max(lo, i * size), min(hi, (i + 1) * size)
        if a < b:
            pieces.append(block[a - i * size : b - i * size])
    return pieces[0] if len(pieces) == 1 else jnp.concatenate(pieces)


def cut_padded(blocks, lo, hi, plan):
    pieces = []
    while lo < hi:
        end = min(hi, (lo // plan.rows + 1) * plan.rows)
        pieces.append(cut(blocks, plan.padded(lo), plan.padded(lo) + end - lo))
        lo = end
    return pieces[0] if len(pieces) == 1 else jnp.concatenate(pieces)


def matrix_of(blocks, lo, shape, plan):
    rows, width = shape
    first = plan.padded(lo)
    last = plan.padded(lo + rows * (width // LANES) - 1) + 1
    a, b = first // plan.block, (last - 1) // plan.block
    if a == b:
        return unflatten(blocks[a], a * plan.block, lo, rows, width, plan)
    base = first // 16 * 16
    return unflatten(cut(blocks, base, round_up(last, 16)), base, lo, rows, width, plan)


def stats(v):
    center = v - jnp.mean(v, axis=-1, keepdims=True)
    scale = lax.rsqrt(jnp.mean(center * center, axis=-1, keepdims=True) + EPS)
    return center * scale, scale


def norm_back(hat, scale, gain, grad):
    inner = grad * gain
    back = scale * (
        inner
        - jnp.mean(inner, axis=-1, keepdims=True)
        - hat * jnp.mean(inner * hat, axis=-1, keepdims=True)
    )
    return back, jnp.sum(grad * hat, axis=0), jnp.sum(grad, axis=0)


def product_back(grad_rows, weight):
    return lax.dot_general(grad_rows, weight, (((1,), (1,)), ((), ())), preferred_element_type=F32)


def weight_grad(lefts, grads):
    return dot_l(jnp.concatenate(lefts), jnp.concatenate(grads))


def row_sum(grads):
    return sum(jnp.sum(g.astype(F32), axis=0) for g in grads)


def add_up(parts):
    total = parts[0]
    for part in parts[1:]:
        total = total + part
    return total


def gelu_pair(u):
    half = 0.5 * (1.0 + lax.erf(u * (2.0 ** -0.5)))
    slope = half + u * jnp.exp(-0.5 * u * u) * ((2.0 * math.pi) ** -0.5)
    return (u * half).astype(BF), slope


def bias_row(q_bias, v_bias):
    return jnp.concatenate([q_bias, jnp.zeros_like(q_bias), v_bias])


def shards(inputs, cotangent, params, clip_counts, slot_live):
    micro, clips, frames, places, d = inputs.shape
    n_sp = lax.axis_size("sp")
    n_dev = lax.axis_size("dp") * n_sp
    full_length = params.shape[0] * n_dev
    tokens = clips * frames * places
    seqs = clips * frames // n_sp
    length = places * n_sp
    rows = params.shape[0] // LANES
    fast = n_sp == 8 and n_dev == 32 and params.shape[0] % (2 * LANES) == 0

    spans, used = segment_rows(d, FF)
    pieces = []
    if fast:
        plan, pos = Plan(rows), place_of()
        blocks = gather_blocks(params, plan, pos)
        for lo, hi, shape in spans:
            lo, hi = lo // LANES, hi // LANES
            if len(shape) == 1:
                pieces.append(cut_padded(blocks, lo, hi, plan).reshape(shape).astype(F32))
            else:
                pieces.append(matrix_of(blocks, lo, shape, plan))
    else:
        blocks = [lax.all_gather(params, BOTH, axis=0, tiled=True).reshape(-1, LANES)]
        for lo, hi, shape in spans:
            piece = cut(blocks, lo // LANES, hi // LANES).reshape(shape)
            pieces.append(piece.astype(F32) if len(shape) == 1 else piece)
    (tg, tb, w_qkv_t, bq_t, bv_t, w_out_t, bo_t, w_fc, b_fc,
     sg, sb, w_qkv_s, bq_s, bv_s, w_out_s, bo_s,
     mg, mb_, w_up, b_up, w_down, b_down) = pieces

    in_use = (jnp.arange(clips, dtype=jnp.int32)[None] < clip_counts).astype(F32)
    live = slot_live.astype(F32) * in_use[:, :, None]
    live_low = live.astype(BF)

    def to_frames(rows):
        return lax.all_to_all(
            rows.reshape(clips * frames, places, d), "sp", split_axis=0, concat_axis=1, tiled=True
        )

    def to_places(rows):
        return lax.all_to_all(
            rows.reshape(seqs, length, d), "sp", split_axis=1, concat_axis=0, tiled=True
        ).reshape(clips, frames, places, d)

    place = jnp.arange(frames * places, dtype=jnp.int32) % places
    same = (place[:, None] == place[None]).astype(F32)[None]
    bias_t = bias_row(bq_t, bv_t)
    bias_s = bias_row(bq_s, bv_s)
    span_t = frames * places

    live_sent = jnp.broadcast_to(live_low[:, :, None], (micro, clips, frames, places)).reshape(
        micro, clips * frames, places
    )
    live_frames = lax.all_to_all(live_sent, "sp", split_axis=1, concat_axis=2, tiled=True)
    keep_s = live_frames.astype(F32).reshape(micro, seqs, 1, length)
    cots = [
        to_frames(cotangent[m] * live_low[m, :, None, :, None]).reshape(seqs * length, d)
        for m in range(micro)
    ]

    time_kept, sent = [], []
    for m in range(micro):
        x = inputs[m].reshape(tokens, d).astype(F32)
        hat, scale = stats(x)
        h1 = (hat * tg + tb).astype(BF)
        qkv = (dot(h1, w_qkv_t) + bias_t).astype(BF)
        o = attend(qkv.reshape(clips, span_t, 3 * d), same, d).reshape(tokens, d)
        a = (dot(o, w_out_t) + bo_t).astype(BF)
        x1 = (x + dot(a, w_fc) + b_fc).astype(BF)
        sent.append(to_frames(x1).reshape(seqs * length, d))
        time_kept.append((h1, qkv, o, a))

    outs, returned, space_kept = [], [], []
    for m in range(micro):
        xb = sent[m].astype(F32)
        hat2, scale2 = stats(xb)
        h2 = (hat2 * sg + sb).astype(BF)
        qkv = (dot(h2, w_qkv_s) + bias_s).astype(BF)
        qkv3 = qkv.reshape(seqs, length, 3 * d)
        o = attend(qkv3, keep_s[m], d).reshape(-1, d)
        x2 = xb + dot(o, w_out_s) + bo_s
        hat3, scale3 = stats(x2)
        h3 = (hat3 * mg + mb_).astype(BF)
        g, slope = gelu_pair(dot(h3, w_up) + b_up)
        x3 = (x2 + dot(g, w_down) + b_down).astype(BF)
        outs.append(to_places(x3) * live_low[m, :, None, :, None])
        dx3 = cots[m]
        du = (product_back(dx3, w_down) * slope).astype(BF)
        back3, d_mg, d_mb = norm_back(hat3, scale3, mg, product_back(du, w_up))
        dx2 = dx3.astype(F32) + back3
        da = dx2.astype(BF)
        do = product_back(da, w_out_s).astype(BF)
        dqkv = [t.reshape(-1, d) for t in attend_back(qkv3, keep_s[m], do.reshape(seqs, length, d), d)]
        dqkv = jnp.concatenate(dqkv, axis=-1)
        back2, d_sg, d_sb = norm_back(hat2, scale2, sg, product_back(dqkv, w_qkv_s))
        dx1 = (dx2 + back2).astype(BF)
        returned.append(to_places(dx1).reshape(tokens, d))
        space_kept.append((h2, dqkv, o, da, h3, du, g, dx3, d_mg, d_mb, d_sg, d_sb))
    (h2s, dqkvs, os_, das, h3s, dus, gs, dx3s, d_mg, d_mb, d_sg, d_sb) = zip(*space_kept)
    grad_down, grad_b_down = weight_grad(gs, dx3s), row_sum(dx3s)
    grad_up, grad_b_up = weight_grad(h3s, dus), row_sum(dus)
    grad_out_s, grad_bo_s = weight_grad(os_, das), row_sum(das)
    grad_qkv_s, sums_s = weight_grad(h2s, dqkvs), row_sum(dqkvs)
    late = [add_up(d_sg), add_up(d_sb), grad_qkv_s, sums_s[:d], sums_s[2 * d :], grad_out_s, grad_bo_s,
            add_up(d_mg), add_up(d_mb), grad_up, grad_b_up, grad_down, grad_b_down]

    input_grads, back_kept = [], []
    for m in range(micro):
        h1, qkv, o, a = time_kept[m]
        dx1 = returned[m]
        da = product_back(dx1, w_fc).astype(BF)
        do = product_back(da, w_out_t).astype(BF)
        dqkv = attend_back(qkv.reshape(clips, span_t, 3 * d), same, do.reshape(clips, span_t, d), d)
        dqkv = jnp.concatenate([t.reshape(tokens, d) for t in dqkv], axis=-1)
        hat, scale = stats(inputs[m].reshape(tokens, d).astype(F32))
        back1, d_tg, d_tb = norm_back(hat, scale, tg, product_back(dqkv, w_qkv_t))
        input_grads.append((dx1.astype(F32) + back1).astype(BF).reshape(clips, frames, places, d))
        back_kept.append((h1, dqkv, o, da, a, dx1, d_tg, d_tb))
    h1s, dqkvs, os_, das, as_, dx1s, d_tg, d_tb = zip(*back_kept)
    grad_fc, grad_b_fc = weight_grad(as_, dx1s), row_sum(dx1s)
    grad_out_t, grad_bo_t = weight_grad(os_, das), row_sum(das)
    grad_qkv_t, sums_t = weight_grad(h1s, dqkvs), row_sum(dqkvs)
    early = [add_up(d_tg), add_up(d_tb), grad_qkv_t, sums_t[:d], sums_t[2 * d :], grad_out_t, grad_bo_t,
             grad_fc, grad_b_fc]

    grads = early + late
    if fast:
        size = 8 * rows
        quarters = [None] * 4
        items, vec_at, vec_parts = [], None, []
        tail = jnp.zeros((full_length - used,), F32)
        for (lo, hi, shape), grad in zip(spans + [(used, full_length, (full_length - used,))], grads + [tail]):
            if len(shape) == 2:
                if vec_parts:
                    items.append((vec_at, jnp.concatenate(vec_parts).reshape(-1, LANES)))
                vec_parts = []
                items.append((lo // LANES, grad))
            else:
                vec_at = vec_at if vec_parts else lo // LANES
                vec_parts.append(grad)
        items.append((vec_at, jnp.concatenate(vec_parts).reshape(-1, LANES)))
        for b in (3, 2, 1, 0):
            mats, vecs = [], []
            for lo, value in items:
                n = value.size // LANES
                if lo < (b + 1) * size and lo + n > b * size:
                    (vecs if value.shape[1] == LANES else mats).append((lo, value))
            quarters[b] = reduce_block(*flatten(pos, b, mats, vecs, plan))
        param_grad = return_quarters(quarters, plan, pos)
    else:
        flat = jnp.concatenate([g.reshape(-1) for g in grads])
        flat = jnp.concatenate([flat, jnp.zeros((full_length - used,), F32)])
        param_grad = lax.psum_scatter(flat, BOTH, scatter_dimension=0, tiled=True)
    return (jnp.stack(outs), jnp.stack(input_grads), param_grad)


def solution(mesh):
    tokens = P(None, "dp", None, "sp", None)
    return jax.shard_map(
        shards,
        mesh=mesh,
        in_specs=(tokens, tokens, P(BOTH), P(None, "dp"), P(None, "dp", "sp")),
        out_specs=(tokens, tokens, P(BOTH)),
        check_vma=False,
    )
```

```python
import math

import jax
import jax.numpy as jnp
from jax import lax
from jax.experimental import pallas as pl
from jax.experimental.pallas import tpu as pltpu
from jax.sharding import PartitionSpec as P

H = 12
FF = 3072
EPS = 1e-06
MASKED = -1000000000.0
LANES = 128
BOTH = ("dp", "sp")
BF = jnp.bfloat16
F32 = jnp.float32


def segment_shapes(d, ff):
    return [
        (d,), (d,), (d, 3 * d), (d,), (d,), (d, d), (d,), (d, d), (d,),
        (d,), (d,), (d, 3 * d), (d,), (d,), (d, d), (d,),
        (d,), (d,), (d, ff), (ff,), (ff, d), (d,),
    ]


def pair_masks(rows):
    lane = lax.broadcasted_iota(jnp.int32, (rows, LANES), 1)
    return lane < LANES // 2


def dot_l(a, b):
    return lax.dot_general(a, b, (((0,), (0,)), ((), ())), preferred_element_type=F32)


def dot(a, b):
    return jnp.dot(a, b, preferred_element_type=F32)


def turn(t):
    return jnp.transpose(t.astype(F32)).astype(BF)


def halves(t):
    half = LANES // 2
    zero = jnp.zeros_like(t[:half])
    return jnp.concatenate([t[:half], zero]), jnp.concatenate([zero, t[half:]])


def exp_of(k, q_turned, keep):
    s = jnp.where(keep, dot(k, q_turned), MASKED)
    e = jnp.exp(s - jnp.max(s, axis=0, keepdims=True))
    return e, 1.0 / jnp.sum(e, axis=0, keepdims=True)


def softmax_of(q, k, keep):
    s = lax.dot_general(q, k, (((1,), (1,)), ((), ())), preferred_element_type=F32)
    s = jnp.where(keep, s, MASKED)
    e = jnp.exp(s - jnp.max(s, axis=-1, keepdims=True))
    return e.astype(BF), 1.0 / jnp.sum(e, axis=-1, keepdims=True)


def attend_kernel(q_ref, k_ref, v_ref, m_ref, o_ref):
    rows, width = q_ref.shape[1], q_ref.shape[2]
    keep = m_ref[0] > 0.5
    first = pair_masks(rows)
    for at in range(0, width, LANES):
        q = q_ref[0, :, at : at + LANES] * jnp.asarray(0.125, BF)
        k = k_ref[0, :, at : at + LANES]
        v = v_ref[0, :, at : at + LANES]
        zero = jnp.zeros_like(q)
        ea, scale_a = softmax_of(jnp.where(first, q, zero), k, keep)
        eb, scale_b = softmax_of(jnp.where(first, zero, q), k, keep)
        o_ref[0, :, at : at + LANES] = jnp.where(first, dot(ea, v) * scale_a, dot(eb, v) * scale_b).astype(BF)


def attend_back_kernel(q_ref, k_ref, v_ref, m_ref, d_ref, o_ref):
    rows, width = q_ref.shape[1], q_ref.shape[2]
    d_model = o_ref.shape[2] // 3
    keep = jnp.broadcast_to(m_ref[0], (rows, rows)) > 0.5
    half = LANES // 2
    first = pair_masks(rows)
    for at in range(0, width, LANES):
        q = q_ref[0, :, at : at + LANES] * jnp.asarray(0.125, BF)
        k = k_ref[0, :, at : at + LANES]
        v = v_ref[0, :, at : at + LANES]
        d = d_ref[0, :, at : at + LANES]
        k_turned = turn(k)
        qs, ds_ = halves(turn(q)), halves(turn(d))
        dqs, dks, dvs = [], [], []
        for head in range(2):
            e, scale = exp_of(k, qs[head], keep)
            p = e * scale
            dp = dot(v, ds_[head])
            ds = (p * (dp - jnp.sum(p * dp, axis=0, keepdims=True))).astype(BF)
            dqs.append(dot(k_turned[head * half : (head + 1) * half], ds))
            dks.append(dot(ds, q))
            dvs.append(dot(p.astype(BF), d))
        results = (
            jnp.transpose(jnp.concatenate(dqs) * 0.125),
            jnp.where(first, *dks),
            jnp.where(first, *dvs),
        )
        for third, result in enumerate(results):
            to = pl.multiple_of(third * d_model + pl.program_id(1) * width + at, LANES)
            o_ref[0, :, pl.ds(to, LANES)] = result.astype(BF)


def head_split(width):
    for parts in (2, 3, 1):
        if width % (parts * LANES) == 0:
            return parts
    return 1


def attention_specs(packed, keep, d):
    parts = head_split(d)
    w = d // parts
    rows = packed.shape[1]
    own = lambda third: pl.BlockSpec((1, rows, w), lambda i, j: (i, 0, third * parts + j))
    one = keep.shape[0] == 1
    mask = pl.BlockSpec((1,) + keep.shape[1:], lambda i, j: (0 if one else i, 0, 0))
    flat = pl.BlockSpec((1, rows, w), lambda i, j: (i, 0, j))
    return parts, own, mask, flat


def attend(packed, keep, d):
    n, rows, _ = packed.shape
    parts, own, mask, flat = attention_specs(packed, keep, d)
    return pl.pallas_call(
        attend_kernel,
        grid=(n, parts),
        in_specs=[own(0), own(1), own(2), mask],
        out_specs=flat,
        out_shape=jax.ShapeDtypeStruct((n, rows, d), BF),
        cost_estimate=pl.CostEstimate(
            flops=4 * n * rows * rows * d * 2,
            bytes_accessed=n * rows * d * 8,
            transcendentals=n * rows * rows * (d // 64),
        ),
        name="attend",
    )(packed, packed, packed, keep)


def attend_back(packed, keep, grad, d):
    n, rows, _ = packed.shape
    parts, own, mask, flat = attention_specs(packed, keep, d)
    return pl.pallas_call(
        attend_back_kernel,
        grid=(n, parts),
        in_specs=[own(0), own(1), own(2), mask, flat],
        out_specs=pl.BlockSpec((1, rows, 3 * d), lambda i, j: (i, 0, 0)),
        out_shape=jax.ShapeDtypeStruct((n, rows, 3 * d), BF),
        cost_estimate=pl.CostEstimate(
            flops=10 * n * rows * rows * d * 2,
            bytes_accessed=n * rows * d * 14,
            transcendentals=n * rows * rows * (d // 64),
        ),
        name="attend_back",
    )(packed, packed, packed, keep, grad)


def flip_perm(dp_bits=0, sp_bits=0):
    return [(d * 8 + s, (d ^ dp_bits) * 8 + (s ^ sp_bits)) for d in range(4) for s in range(8)]


def send(value, dp_bits=0, sp_bits=0):
    return lax.ppermute(value, BOTH, flip_perm(dp_bits, sp_bits))


def pick(stack, at):
    return lax.dynamic_index_in_dim(stack, at, 0, keepdims=False)


def place_of():
    dp, sp = lax.axis_index("dp"), lax.axis_index("sp")
    return jnp.stack([dp, sp >> 1, sp & 1]).astype(jnp.int32)


def round_up(value, step):
    return -(-value // step) * step


class Plan:
    def __init__(self, rows):
        self.rows = rows
        self.part = round_up(-(-rows // 4), 16)
        self.gap = 4 * self.part - rows
        self.block = 32 * self.part

    def padded(self, row):
        return row + self.gap * (row // self.rows)


def assemble_kernel(pos_ref, *refs):
    ins, out, buf, sem_in, sem_out = refs[:8], refs[8], refs[9], refs[10], refs[11]
    dp, z, core = pos_ref[0], pos_ref[1], pos_ref[2]
    loads = []
    for j in range(8):
        for k in range(4):
            at = j * 4 + k
            load = pltpu.make_async_copy(ins[j].at[k], buf.at[at], sem_in.at[at])
            load.start()
            loads.append(load)
    stores = []
    for j in range(8):
        for k in range(4):
            at = j * 4 + k
            loads[at].wait()
            to = ((z ^ k) * 2 + (core ^ (j // 4))) * 4 + (dp ^ (j % 4))
            store = pltpu.make_async_copy(buf.at[at], out.at[to], sem_out.at[at])
            store.start()
            stores.append(store)
    for store in stores:
        store.wait()


def assemble(pos, pieces):
    part = pieces[0].shape[1]
    any_spec = pl.BlockSpec(memory_space=pl.ANY)
    out = pl.pallas_call(
        assemble_kernel,
        grid_spec=pltpu.PrefetchScalarGridSpec(
            num_scalar_prefetch=1,
            grid=(1,),
            in_specs=[any_spec] * 8,
            out_specs=any_spec,
            scratch_shapes=[
                pltpu.VMEM((32, part, LANES), BF),
                pltpu.SemaphoreType.DMA((32,)),
                pltpu.SemaphoreType.DMA((32,)),
            ],
        ),
        out_shape=jax.ShapeDtypeStruct((32, part, LANES), BF),
        cost_estimate=pl.CostEstimate(flops=0, bytes_accessed=32 * part * LANES * 4, transcendentals=0),
        name="assemble",
    )(pos, *pieces)
    return out.reshape(32 * part, LANES)


def tie(*values):
    return lax.optimization_barrier(values)


class Gather:
    SCHEDULE = (
        ((0, 0),),
        ((0, 1), (1, 0)),
        ((0, 2), (2, 0)),
        ((0, 3), (1, 1), (3, 0)),
        ((1, 2), (2, 1)),
        ((1, 3), (2, 2), (3, 1)),
        ((2, 3), (3, 2)),
        ((3, 3),),
    )

    def __init__(self, shard, plan, pos):
        self.plan, self.pos = plan, pos
        dp = pos[0]
        mine = jnp.pad(shard.reshape(plan.rows, LANES), ((0, plan.gap), (0, 0)))
        mine = mine.reshape(4, plan.part, LANES)
        spread = jnp.zeros_like(mine)
        for k in range(4):
            piece = pick(mine, dp ^ k)
            got = piece if k == 0 else send(piece, k)
            spread = lax.dynamic_update_slice(spread, got[None], (dp ^ k, 0, 0))
        self.state = [[spread[b]] for b in range(4)]
        self.stage_number = 0

    def stage(self):
        for b, step in self.SCHEDULE[self.stage_number]:
            now = self.state[b]
            if step == 0:
                now = now + [send(now[0], 0, 2 * k) for k in range(1, 4)]
            elif step == 1:
                line = jnp.stack(now)
                now = [line, send(line, 1), send(line, 2)]
            elif step == 2:
                line, by_x, by_y = now
                now = [line, by_x, by_y, jnp.concatenate([send(by_x[:2], 2), send(by_y[2:], 1)])]
            else:
                now = now + [send(part, 0, 1) for part in now]
            self.state[b] = now
        self.stage_number += 1

    def sync(self, *values):
        self.state, values = tie(self.state, values)
        return values

    def block(self, b):
        return assemble(self.pos, self.state[b])


CHUNK = 1152


def unflatten(src, base, off, rows, width, plan):
    lanes = width // LANES
    step_rows = CHUNK // lanes
    size = src.shape[0]
    window = round_up(CHUNK + plan.gap + 16, 16)

    def where_from(i):
        first = off + CHUNK * i
        at = first + plan.gap * (first // plan.rows) - base
        return first, at, jnp.minimum(at // 16 * 16, size - window)

    def kernel(in_ref, out_ref, wide):
        first, at, start = where_from(pl.program_id(0))
        delta = at - start
        left = plan.rows - first % plan.rows
        wide[...] = in_ref[...].astype(F32)

        @pl.when(left >= CHUNK)
        def _():
            for b in range(lanes):
                got = wide[pl.ds(delta + b, step_rows, stride=lanes), :]
                out_ref[:, b * LANES : (b + 1) * LANES] = got.astype(BF)

        @pl.when(left < CHUNK)
        def _():
            row = lax.broadcasted_iota(jnp.int32, (step_rows, LANES), 0) * lanes
            for b in range(lanes):
                near = wide[pl.ds(delta + b, step_rows, stride=lanes), :]
                far = wide[pl.ds(delta + b + plan.gap, step_rows, stride=lanes), :]
                got = jnp.where(row + b < left, near, far)
                out_ref[:, b * LANES : (b + 1) * LANES] = got.astype(BF)

    return pl.pallas_call(
        kernel,
        grid=(rows // step_rows,),
        in_specs=[
            pl.BlockSpec(
                (pl.Element(window), pl.Element(LANES)),
                lambda i: (pl.multiple_of(where_from(i)[2], 16), 0),
            )
        ],
        out_specs=pl.BlockSpec((step_rows, width), lambda i: (i, 0)),
        out_shape=jax.ShapeDtypeStruct((rows, width), BF),
        scratch_shapes=[pltpu.VMEM((window, LANES), F32)],
        cost_estimate=pl.CostEstimate(flops=0, bytes_accessed=rows * width * 4, transcendentals=0),
        name="unflatten",
    )(src)


def flatten(pos, b, mats, vecs, plan):
    part, span = plan.part, plan.rows
    shapes = []
    for off, mat in mats:
        lanes = mat.shape[1] // LANES
        shapes.append((off, mat.shape[0], lanes, round_up(-(-span // lanes) + 8, 8)))
    pad = round_up(max([w * c for _, _, c, w in shapes] + [v.shape[0] for _, v in vecs]), 8) + 8

    def first_row(t, pos_ref):
        z = pos_ref[1] ^ (t % 4)
        core = jnp.where(t < 4, 1 - pos_ref[2], pos_ref[2])
        return (8 * b + z * 2 + core) * span

    def start_row(p0, off, rows, lanes, w):
        return jnp.minimum(jnp.maximum(p0 - off, 0) // lanes // 8 * 8, rows - w)

    def kernel(pos_ref, *refs):
        ins = refs[: len(mats)]
        vins = refs[len(mats) : len(mats) + len(vecs)]
        theirs, ours, wide = refs[len(mats) + len(vecs) :]
        t = pl.program_id(0)
        p0 = first_row(t, pos_ref)
        for (off, rows, lanes, w), ref in zip(shapes, ins):

            @pl.when((p0 + span > off) & (p0 < off + rows * lanes))
            def _():
                at = off + lanes * start_row(p0, off, rows, lanes, w) - p0 + pad
                for c in range(lanes):
                    wide[pl.ds(at + c, w, stride=lanes), :] = ref[:, c * LANES : (c + 1) * LANES]

        for (off, vec), ref in zip(vecs, vins):
            n = vec.shape[0]

            @pl.when((p0 + span > off) & (p0 < off + n))
            def _():
                at = off - p0 + pad
                for r in range(n):
                    wide[pl.ds(at + r, 1), :] = ref[r : r + 1, :]

        for out, mine in ((theirs, t < 4), (ours, t >= 4)):

            @pl.when(mine)
            def _():
                for k in range(4):
                    at = pl.multiple_of(pad + (pos_ref[0] ^ k) * part, 8)
                    out[k, 0] = wide[pl.ds(at, part), :].astype(BF)

    in_specs = [
        pl.BlockSpec(
            (pl.Element(w), pl.Element(lanes * LANES)),
            lambda t, p, off=off, rows=rows, lanes=lanes, w=w: (
                pl.multiple_of(start_row(first_row(t, p), off, rows, lanes, w), 8),
                0,
            ),
        )
        for off, rows, lanes, w in shapes
    ] + [pl.BlockSpec(v.shape, lambda t, p: (0, 0)) for _, v in vecs]
    shape = jax.ShapeDtypeStruct((4, 4, part, LANES), BF)
    return pl.pallas_call(
        kernel,
        grid_spec=pltpu.PrefetchScalarGridSpec(
            num_scalar_prefetch=1,
            grid=(8,),
            in_specs=in_specs,
            out_specs=[
                pl.BlockSpec((4, 1, part, LANES), lambda t, p: (0, jnp.minimum(t, 3), 0, 0)),
                pl.BlockSpec((4, 1, part, LANES), lambda t, p: (0, jnp.maximum(t - 4, 0), 0, 0)),
            ],
            scratch_shapes=[pltpu.VMEM((2 * pad + 4 * part, LANES), F32)],
        ),
        out_shape=[shape, shape],
        cost_estimate=pl.CostEstimate(flops=0, bytes_accessed=plan.block * LANES * 6, transcendentals=0),
        name="flatten",
    )(pos, *[m for _, m in mats], *[v for _, v in vecs])


class Reduce:
    def __init__(self, theirs, ours):
        self.state = (theirs, ours)
        self.stage_number = 0

    def stage(self):
        s, now = self.stage_number, self.state
        wide = lambda *parts: sum(p.astype(F32) for p in parts)
        if s == 0:
            theirs, ours = now
            self.state = (ours, send(theirs, 0, 1))
        elif s == 1:
            ours = wide(*now).astype(BF)
            self.state = (ours, send(ours[3, :2], 1), send(ours[3, 2:], 2))
        elif s == 2:
            ours, by_x, by_y = now
            to_x = jnp.concatenate([ours[1, :2], wide(ours[1, 2:], by_y).astype(BF)])
            to_y = jnp.concatenate([wide(ours[2, :2], by_x).astype(BF), ours[2, 2:]])
            self.state = (ours[0], send(to_x, 1), send(to_y, 2))
        elif s == 3:
            line = wide(*now).astype(BF)
            self.state = (line[0],) + tuple(send(line[k], 0, 2 * k) for k in range(1, 4))
        else:
            self.state = wide(*now)
        self.stage_number = s + 1


def advance(reduces, *values):
    states, values = tie([r.state for r in reduces], values)
    for r, state in zip(reduces, states):
        r.state = state
        r.stage()
    return values


def return_quarters(quarters, plan, pos):
    stack = jnp.stack(quarters)
    dp = pos[0]
    out = jnp.zeros_like(stack)
    for k in range(4):
        piece = pick(stack, dp ^ k)
        got = piece if k == 0 else send(piece, k)
        out = lax.dynamic_update_slice(out, got[None], (dp ^ k, 0, 0))
    return out.reshape(4 * plan.part, LANES)[: plan.rows].reshape(-1)


def segment_rows(d, ff):
    spans, at = [], 0
    for shape in segment_shapes(d, ff):
        length = math.prod(shape)
        spans.append((at, at + length, shape))
        at += length
    return spans, at


def cut(blocks, lo, hi):
    size = blocks[0].shape[0]
    pieces = []
    for i, block in enumerate(blocks):
        a, b = max(lo, i * size), min(hi, (i + 1) * size)
        if a < b:
            pieces.append(block[a - i * size : b - i * size])
    return pieces[0] if len(pieces) == 1 else jnp.concatenate(pieces)


def cut_padded(blocks, lo, hi, plan):
    pieces = []
    while lo < hi:
        end = min(hi, (lo // plan.rows + 1) * plan.rows)
        pieces.append(cut(blocks, plan.padded(lo), plan.padded(lo) + end - lo))
        lo = end
    return pieces[0] if len(pieces) == 1 else jnp.concatenate(pieces)


def matrix_of(blocks, lo, shape, plan):
    rows, width = shape
    first = plan.padded(lo)
    last = plan.padded(lo + rows * (width // LANES) - 1) + 1
    a, b = first // plan.block, (last - 1) // plan.block
    if a == b:
        return unflatten(blocks[a], a * plan.block, lo, rows, width, plan)
    base = first // 16 * 16
    return unflatten(cut(blocks, base, round_up(last, 16)), base, lo, rows, width, plan)


def stats(v):
    center = v - jnp.mean(v, axis=-1, keepdims=True)
    scale = lax.rsqrt(jnp.mean(center * center, axis=-1, keepdims=True) + EPS)
    return center * scale, scale


def norm_back(hat, scale, gain, grad):
    inner = grad * gain
    back = scale * (
        inner
        - jnp.mean(inner, axis=-1, keepdims=True)
        - hat * jnp.mean(inner * hat, axis=-1, keepdims=True)
    )
    return back, jnp.sum(grad * hat, axis=0), jnp.sum(grad, axis=0)


def product_back(grad_rows, weight):
    return lax.dot_general(grad_rows, weight, (((1,), (1,)), ((), ())), preferred_element_type=F32)


def row_sum(grad):
    return jnp.sum(grad.astype(F32), axis=0)


def gelu_pair(u):
    half = 0.5 * (1.0 + lax.erf(u * (2.0 ** -0.5)))
    slope = half + u * jnp.exp(-0.5 * u * u) * ((2.0 * math.pi) ** -0.5)
    return (u * half).astype(BF), slope


def bias_row(q_bias, v_bias):
    return jnp.concatenate([q_bias, jnp.zeros_like(q_bias), v_bias])


def shards(inputs, cotangent, params, clip_counts, slot_live):
    micro, clips, frames, places, d = inputs.shape
    n_sp = lax.axis_size("sp")
    n_dev = lax.axis_size("dp") * n_sp
    full_length = params.shape[0] * n_dev
    tokens = micro * clips * frames * places
    seqs = micro * clips * frames // n_sp
    length = places * n_sp
    rows = params.shape[0] // LANES
    fast = n_sp == 8 and n_dev == 32 and params.shape[0] % (2 * LANES) == 0
    spans, used = segment_rows(d, FF)
    inputs_now, cot_now, live_now = inputs, cotangent, slot_live

    if fast:
        plan, pos = Plan(rows), place_of()
        blocks = [None] * 4
        made = {}

        def piece(i):
            if i not in made:
                lo, hi, shape = spans[i]
                if len(shape) == 1:
                    made[i] = cut_padded(blocks, lo // LANES, hi // LANES, plan).reshape(shape).astype(F32)
                else:
                    made[i] = matrix_of(blocks, lo // LANES, shape, plan)
            return made[i]

        gather = Gather(params, plan, pos)
        for _ in range(4):
            gather.stage()
            cot_now, live_now = gather.sync(cot_now, live_now)
        blocks[0] = gather.block(0)
        gather.stage()
        made[2], made[5] = gather.sync(piece(2), piece(5))
        gather.stage()
    else:
        flat = lax.all_gather(params, BOTH, axis=0, tiled=True).reshape(-1, LANES)

        def piece(i):
            lo, hi, shape = spans[i]
            got = flat[lo // LANES : hi // LANES].reshape(shape)
            return got.astype(F32) if len(shape) == 1 else got

    in_use = (jnp.arange(clips, dtype=jnp.int32)[None] < clip_counts).astype(F32)
    live = live_now.astype(F32) * in_use[:, :, None]
    live_low = live.astype(BF)[:, :, None, :, None]

    def to_frames(value):
        return lax.all_to_all(
            value.reshape(micro, clips * frames, places, d), "sp", split_axis=1, concat_axis=2, tiled=True
        ).reshape(seqs * length, d)

    def to_places(value):
        return lax.all_to_all(
            value.reshape(micro, seqs // micro, length, d), "sp", split_axis=2, concat_axis=1, tiled=True
        ).reshape(micro, clips, frames, places, d)

    live_sent = jnp.broadcast_to(live.astype(BF)[:, :, None], (micro, clips, frames, places)).reshape(
        micro, clips * frames, places
    )
    live_frames = lax.all_to_all(live_sent, "sp", split_axis=1, concat_axis=2, tiled=True)
    keep_rows = live_frames.astype(F32).reshape(seqs, 1, length)
    keep_s = keep_rows.reshape(seqs, length, 1)
    dx3 = to_frames(cot_now * live_low)

    span_t = frames * places
    place = jnp.arange(span_t, dtype=jnp.int32) % places
    same = (place[:, None] == place[None]).astype(F32)[None]

    x = inputs_now.reshape(tokens, d).astype(F32)
    hat1, scale1 = stats(x)
    tg = piece(0)
    h1 = (hat1 * tg + piece(1)).astype(BF)
    w_qkv_t = piece(2)
    qkv_t = (dot(h1, w_qkv_t) + bias_row(piece(3), piece(4))).astype(BF)
    qkv_t = qkv_t.reshape(micro * clips, span_t, 3 * d)
    if fast:
        (qkv_t,) = gather.sync(qkv_t)
        gather.stage()
    o_t = attend(qkv_t, same, d).reshape(tokens, d)
    if fast:
        o_t, dx3 = gather.sync(o_t, dx3)
        gather.stage()
        blocks[1] = gather.block(1)
    w_out_t = piece(5)
    a_t = (dot(o_t, w_out_t) + piece(6)).astype(BF)
    w_fc = piece(7)
    x1 = (x + dot(a_t, w_fc) + piece(8)).astype(BF)
    if fast:
        (x1,) = gather.sync(x1)
    xb = to_frames(x1)
    if fast:
        blocks[2], blocks[3] = gather.block(2), gather.block(3)

    w_qkv_s, w_out_s, w_up, w_down = piece(11), piece(14), piece(18), piece(20)
    if fast:
        xb, w_qkv_s, w_out_s, w_up, w_down = tie(xb, w_qkv_s, w_out_s, w_up, w_down)
    xb = xb.astype(F32)
    hat2, scale2 = stats(xb)
    sg = piece(9)
    h2 = (hat2 * sg + piece(10)).astype(BF)
    qkv_s = (dot(h2, w_qkv_s) + bias_row(piece(12), piece(13))).astype(BF)
    qkv_s = qkv_s.reshape(seqs, length, 3 * d)
    o_s = attend(qkv_s, keep_rows, d).reshape(-1, d)
    x2 = xb + dot(o_s, w_out_s) + piece(15)
    hat3, scale3 = stats(x2)
    mg = piece(16)
    h3 = (hat3 * mg + piece(17)).astype(BF)
    g, slope = gelu_pair(dot(h3, w_up) + piece(19))
    x3 = (x2 + dot(g, w_down) + piece(21)).astype(BF)
    out = to_places(x3) * live_low

    du = (product_back(dx3, w_down) * slope).astype(BF)
    back3, grad_mg, grad_mb = norm_back(hat3, scale3, mg, product_back(du, w_up))
    dx2 = dx3.astype(F32) + back3
    da_s = dx2.astype(BF)
    do_s = product_back(da_s, w_out_s).astype(BF)
    dqkv_s = attend_back(qkv_s, keep_s, do_s.reshape(seqs, length, d), d).reshape(-1, 3 * d)
    back2, grad_sg, grad_sb = norm_back(hat2, scale2, sg, product_back(dqkv_s, w_qkv_s))
    dx1 = to_places((dx2 + back2).astype(BF)).reshape(tokens, d)

    grads = [None] * len(spans)
    grads[20], grads[21] = dot_l(g, dx3), row_sum(dx3)
    grads[18], grads[19] = dot_l(h3, du), row_sum(du)
    grads[14], grads[15] = dot_l(o_s, da_s), row_sum(da_s)
    grads[16], grads[17] = grad_mg, grad_mb
    grads[9], grads[10] = grad_sg, grad_sb

    def block_of(b):
        size = 8 * rows
        tail = jnp.zeros((full_length - used,), F32)
        mats, vecs, run, run_at = [], [], [], 0
        for i, (lo, hi, shape) in enumerate(spans + [(used, full_length, (full_length - used,))]):
            inside = lo < (b + 1) * size * LANES and hi > b * size * LANES
            if len(shape) == 2 or not inside:
                if run:
                    vecs.append((run_at, jnp.concatenate(run).reshape(-1, LANES)))
                run = []
                if inside:
                    mats.append((lo // LANES, grads[i]))
            else:
                run_at = run_at if run else lo // LANES
                run.append(grads[i] if i < len(grads) else tail)
        if run:
            vecs.append((run_at, jnp.concatenate(run).reshape(-1, LANES)))
        return Reduce(*flatten(pos, b, mats, vecs, plan))

    if fast:
        r3 = block_of(3)
        r3.stage()
        r2 = block_of(2)
        r2.stage()
    grads[11] = dot_l(h2, dqkv_s)
    sums = row_sum(dqkv_s)
    grads[12], grads[13] = sums[:d], sums[2 * d :]
    if fast:
        dx1, grads[11] = advance((r3, r2), dx1, grads[11])

    da_t = product_back(dx1, w_fc).astype(BF)
    do_t = product_back(da_t, w_out_t).astype(BF)
    grads[7], grads[8] = dot_l(a_t, dx1), row_sum(dx1)
    if fast:
        do_t, grads[7] = advance((r3, r2), do_t, grads[7])
        r1 = block_of(1)
        r1.stage()
    dqkv_t = attend_back(qkv_t, same, do_t.reshape(micro * clips, span_t, d), d).reshape(tokens, 3 * d)
    if fast:
        (dqkv_t,) = advance((r3, r2, r1), dqkv_t)
    sums = row_sum(dqkv_t)
    grads[3], grads[4] = sums[:d], sums[2 * d :]
    back1, grads[0], grads[1] = norm_back(hat1, scale1, tg, product_back(dqkv_t, w_qkv_t))
    grads[5], grads[6] = dot_l(o_t, da_t), row_sum(da_t)
    grads[2] = dot_l(h1, dqkv_t)
    input_grad = (dx1.astype(F32) + back1).astype(BF).reshape(inputs.shape)

    if fast:
        (grads[2],) = advance((r3, r2, r1), grads[2])
        r0 = block_of(0)
        r0.stage()
        advance((r1, r0))
        advance((r1, r0))
        advance((r0,))
        advance((r0,))
        param_grad = return_quarters([r0.state, r1.state, r2.state, r3.state], plan, pos)
    else:
        flat = jnp.concatenate([g.reshape(-1) for g in grads] + [jnp.zeros((full_length - used,), F32)])
        param_grad = lax.psum_scatter(flat, BOTH, scatter_dimension=0, tiled=True)
    return (out, input_grad, param_grad)


def solution(mesh):
    tokens = P(None, "dp", None, "sp", None)
    return jax.shard_map(
        shards,
        mesh=mesh,
        in_specs=(tokens, tokens, P(BOTH), P(None, "dp"), P(None, "dp", "sp")),
        out_specs=(tokens, tokens, P(BOTH)),
        check_vma=False,
    )
```

```python
import math

import jax
import jax.numpy as jnp
from jax import lax
from jax.experimental import pallas as pl
from jax.experimental.pallas import tpu as pltpu
from jax.sharding import PartitionSpec as P


FF = 3072
EPS = 1e-06
MASKED = -1000000000.0
LANES = 128
BOTH = ("dp", "sp")
BF = jnp.bfloat16
F32 = jnp.float32


def segment_shapes(d, ff):
    return [
        (d,), (d,), (d, 3 * d), (d,), (d,), (d, d), (d,), (d, d), (d,),
        (d,), (d,), (d, 3 * d), (d,), (d,), (d, d), (d,),
        (d,), (d,), (d, ff), (ff,), (ff, d), (d,),
    ]


def pair_masks(rows):
    lane = lax.broadcasted_iota(jnp.int32, (rows, LANES), 1)
    return lane < LANES // 2


def dot_l(a, b):
    return lax.dot_general(a, b, (((0,), (0,)), ((), ())), preferred_element_type=F32)


def dot(a, b):
    return jnp.dot(a, b, preferred_element_type=F32)


def turn(t):
    return jnp.transpose(t.astype(F32)).astype(BF)


def halves(t):
    half = LANES // 2
    zero = jnp.zeros_like(t[:half])
    return jnp.concatenate([t[:half], zero]), jnp.concatenate([zero, t[half:]])


def exp_of(k, q_turned, keep):
    s = jnp.where(keep, dot(k, q_turned), MASKED)
    e = jnp.exp(s - jnp.max(s, axis=0, keepdims=True))
    return e, 1.0 / jnp.sum(e, axis=0, keepdims=True)


def softmax_of(q, k, keep):
    s = lax.dot_general(q, k, (((1,), (1,)), ((), ())), preferred_element_type=F32)
    s = jnp.where(keep, s, MASKED)
    e = jnp.exp(s - jnp.max(s, axis=-1, keepdims=True))
    return e.astype(BF), 1.0 / jnp.sum(e, axis=-1, keepdims=True)


def attend_kernel(q_ref, k_ref, v_ref, m_ref, o_ref):
    rows, width = q_ref.shape[1], q_ref.shape[2]
    keep = m_ref[0] > 0.5
    first = pair_masks(rows)
    for at in range(0, width, LANES):
        q = q_ref[0, :, at : at + LANES] * jnp.asarray(0.125, BF)
        k = k_ref[0, :, at : at + LANES]
        v = v_ref[0, :, at : at + LANES]
        zero = jnp.zeros_like(q)
        ea, scale_a = softmax_of(jnp.where(first, q, zero), k, keep)
        eb, scale_b = softmax_of(jnp.where(first, zero, q), k, keep)
        o_ref[0, :, at : at + LANES] = jnp.where(first, dot(ea, v) * scale_a, dot(eb, v) * scale_b).astype(BF)


def attend_back_kernel(q_ref, k_ref, v_ref, m_ref, d_ref, o_ref):
    rows, width = q_ref.shape[1], q_ref.shape[2]
    d_model = o_ref.shape[2] // 3
    keep = jnp.broadcast_to(m_ref[0], (rows, rows)) > 0.5
    half = LANES // 2
    first = pair_masks(rows)
    for at in range(0, width, LANES):
        q = q_ref[0, :, at : at + LANES] * jnp.asarray(0.125, BF)
        k = k_ref[0, :, at : at + LANES]
        v = v_ref[0, :, at : at + LANES]
        d = d_ref[0, :, at : at + LANES]
        k_turned = turn(k)
        qs, ds_ = halves(turn(q)), halves(turn(d))
        dqs, dks, dvs = [], [], []
        for head in range(2):
            e, scale = exp_of(k, qs[head], keep)
            p = e * scale
            dp = dot(v, ds_[head])
            ds = (p * (dp - jnp.sum(p * dp, axis=0, keepdims=True))).astype(BF)
            dqs.append(dot(k_turned[head * half : (head + 1) * half], ds))
            dks.append(dot(ds, q))
            dvs.append(dot(p.astype(BF), d))
        results = (
            jnp.transpose(jnp.concatenate(dqs) * 0.125),
            jnp.where(first, *dks),
            jnp.where(first, *dvs),
        )
        for third, result in enumerate(results):
            to = pl.multiple_of(third * d_model + pl.program_id(1) * width + at, LANES)
            o_ref[0, :, pl.ds(to, LANES)] = result.astype(BF)


def head_split(width):
    for parts in (2, 3, 1):
        if width % (parts * LANES) == 0:
            return parts
    return 1


def attention_specs(packed, keep, d):
    parts = head_split(d)
    w = d // parts
    rows = packed.shape[1]
    own = lambda third: pl.BlockSpec((1, rows, w), lambda i, j: (i, 0, third * parts + j))
    one = keep.shape[0] == 1
    mask = pl.BlockSpec((1,) + keep.shape[1:], lambda i, j: (0 if one else i, 0, 0))
    flat = pl.BlockSpec((1, rows, w), lambda i, j: (i, 0, j))
    return parts, own, mask, flat


def attend(packed, keep, d):
    n, rows, _ = packed.shape
    parts, own, mask, flat = attention_specs(packed, keep, d)
    return pl.pallas_call(
        attend_kernel,
        grid=(n, parts),
        in_specs=[own(0), own(1), own(2), mask],
        out_specs=flat,
        out_shape=jax.ShapeDtypeStruct((n, rows, d), BF),
        cost_estimate=pl.CostEstimate(
            flops=4 * n * rows * rows * d * 2,
            bytes_accessed=n * rows * d * 8,
            transcendentals=n * rows * rows * (d // 64),
        ),
        name="attend",
    )(packed, packed, packed, keep)


def attend_back(packed, keep, grad, d):
    n, rows, _ = packed.shape
    parts, own, mask, flat = attention_specs(packed, keep, d)
    return pl.pallas_call(
        attend_back_kernel,
        grid=(n, parts),
        in_specs=[own(0), own(1), own(2), mask, flat],
        out_specs=pl.BlockSpec((1, rows, 3 * d), lambda i, j: (i, 0, 0)),
        out_shape=jax.ShapeDtypeStruct((n, rows, 3 * d), BF),
        cost_estimate=pl.CostEstimate(
            flops=10 * n * rows * rows * d * 2,
            bytes_accessed=n * rows * d * 14,
            transcendentals=n * rows * rows * (d // 64),
        ),
        name="attend_back",
    )(packed, packed, packed, keep, grad)


def flip_perm(dp_bits=0, sp_bits=0):
    return [(d * 8 + s, (d ^ dp_bits) * 8 + (s ^ sp_bits)) for d in range(4) for s in range(8)]


def send(value, dp_bits=0, sp_bits=0):
    return lax.ppermute(value, BOTH, flip_perm(dp_bits, sp_bits))


def pick(stack, at):
    return lax.dynamic_index_in_dim(stack, at, 0, keepdims=False)


def place_of():
    dp, sp = lax.axis_index("dp"), lax.axis_index("sp")
    return jnp.stack([dp, sp >> 1, sp & 1]).astype(jnp.int32)


def round_up(value, step):
    return -(-value // step) * step


class Plan:
    def __init__(self, rows):
        self.rows = rows
        self.part = round_up(-(-rows // 4), 16)
        self.gap = 4 * self.part - rows
        self.block = 32 * self.part

    def padded(self, row):
        return row + self.gap * (row // self.rows)


def assemble_kernel(pos_ref, *refs):
    ins, out, buf, sem_in, sem_out = refs[:8], refs[8], refs[9], refs[10], refs[11]
    dp, z, core = pos_ref[0], pos_ref[1], pos_ref[2]
    loads = []
    for j in range(8):
        for k in range(4):
            at = j * 4 + k
            load = pltpu.make_async_copy(ins[j].at[k], buf.at[at], sem_in.at[at])
            load.start()
            loads.append(load)
    stores = []
    for j in range(8):
        for k in range(4):
            at = j * 4 + k
            loads[at].wait()
            to = ((z ^ k) * 2 + (core ^ (j // 4))) * 4 + (dp ^ (j % 4))
            store = pltpu.make_async_copy(buf.at[at], out.at[to], sem_out.at[at])
            store.start()
            stores.append(store)
    for store in stores:
        store.wait()


def assemble(pos, pieces):
    part = pieces[0].shape[1]
    any_spec = pl.BlockSpec(memory_space=pl.ANY)
    out = pl.pallas_call(
        assemble_kernel,
        grid_spec=pltpu.PrefetchScalarGridSpec(
            num_scalar_prefetch=1,
            grid=(1,),
            in_specs=[any_spec] * 8,
            out_specs=any_spec,
            scratch_shapes=[
                pltpu.VMEM((32, part, LANES), BF),
                pltpu.SemaphoreType.DMA((32,)),
                pltpu.SemaphoreType.DMA((32,)),
            ],
        ),
        out_shape=jax.ShapeDtypeStruct((32, part, LANES), BF),
        cost_estimate=pl.CostEstimate(flops=0, bytes_accessed=32 * part * LANES * 4, transcendentals=0),
        name="assemble",
    )(pos, *pieces)
    return out.reshape(32 * part, LANES)


def tie(*values):
    return lax.optimization_barrier(values)


class Gather:
    SCHEDULE = (
        ((0, 0),),
        ((0, 1), (1, 0)),
        ((0, 2), (2, 0)),
        ((0, 3), (1, 1), (3, 0)),
        ((1, 2), (2, 1)),
        ((1, 3), (2, 2), (3, 1)),
        ((2, 3), (3, 2)),
        ((3, 3),),
    )

    def __init__(self, shard, plan, pos):
        self.plan, self.pos = plan, pos
        dp = pos[0]
        mine = jnp.pad(shard.reshape(plan.rows, LANES), ((0, plan.gap), (0, 0)))
        mine = mine.reshape(4, plan.part, LANES)
        spread = jnp.zeros_like(mine)
        for k in range(4):
            piece = pick(mine, dp ^ k)
            got = piece if k == 0 else send(piece, k)
            spread = lax.dynamic_update_slice(spread, got[None], (dp ^ k, 0, 0))
        self.state = [[spread[b]] for b in range(4)]
        self.stage_number = 0

    def stage(self):
        self.exchange()
        self.stage_number += 1

    def exchange(self):
        for b, step in self.SCHEDULE[self.stage_number]:
            now = self.state[b]
            if step == 0:
                now = now + [send(now[0], 0, 2 * k) for k in range(1, 4)]
            elif step == 1:
                line = jnp.stack(now)
                now = [line, send(line, 1), send(line, 2)]
            elif step == 2:
                line, by_x, by_y = now
                now = [line, by_x, by_y, jnp.concatenate([send(by_x[:2], 2), send(by_y[2:], 1)])]
            else:
                now = now + [send(part, 0, 1) for part in now]
            self.state[b] = now

    def sync(self, *values):
        self.state, values = tie(self.state, values)
        return values

    def block(self, b):
        return assemble(self.pos, self.state[b])


CHUNK = 1152


def unflatten(blocks, a, off, rows, width, plan):
    lanes = width // LANES
    step_rows = CHUNK // lanes
    size = plan.block
    window = round_up(CHUNK + plan.gap + 16, 16)
    two = plan.padded(off + rows * lanes - 1) >= (a + 1) * size

    def where_from(i):
        first = off + CHUNK * i
        at = first + plan.gap * (first // plan.rows) - a * size
        start = jnp.minimum(at // 16 * 16, size - window)
        start_next = jnp.clip((at - size) // 16 * 16, 0, size - window)
        return first, at, start, start_next

    def kernel(*refs):
        in_ref, out_ref, wide = refs[0], refs[-2], refs[-1]
        first, at, start, start_next = where_from(pl.program_id(0))
        left = plan.rows - first % plan.rows
        delta = at - start
        over = delta + plan.gap
        if two:
            delta = jnp.where(at < size, delta, at - size - start_next)
            crossing = (at < size) & (at + left + plan.gap >= size)
            over = jnp.where(crossing, window - left, delta + plan.gap)

            @pl.when(at < size)
            def _():
                wide[:window] = in_ref[...].astype(F32)

            @pl.when(at >= size)
            def _():
                wide[:window] = refs[1][...].astype(F32)

            @pl.when(crossing)
            def _():
                wide[window:] = refs[1][...].astype(F32)

        else:
            wide[:window] = in_ref[...].astype(F32)

        @pl.when(left >= CHUNK)
        def _():
            for b in range(lanes):
                got = wide[pl.ds(delta + b, step_rows, stride=lanes), :]
                out_ref[:, b * LANES : (b + 1) * LANES] = got.astype(BF)

        @pl.when(left < CHUNK)
        def _():
            row = lax.broadcasted_iota(jnp.int32, (step_rows, LANES), 0) * lanes
            for b in range(lanes):
                near = wide[pl.ds(delta + b, step_rows, stride=lanes), :]
                far = wide[pl.ds(over + b, step_rows, stride=lanes), :]
                got = jnp.where(row + b < left, near, far)
                out_ref[:, b * LANES : (b + 1) * LANES] = got.astype(BF)

    element = (pl.Element(window), pl.Element(LANES))
    in_specs = [pl.BlockSpec(element, lambda i: (pl.multiple_of(where_from(i)[2], 16), 0))]
    if two:
        in_specs.append(pl.BlockSpec(element, lambda i: (pl.multiple_of(where_from(i)[3], 16), 0)))
    return pl.pallas_call(
        kernel,
        grid=(rows // step_rows,),
        in_specs=in_specs,
        out_specs=pl.BlockSpec((step_rows, width), lambda i: (i, 0)),
        out_shape=jax.ShapeDtypeStruct((rows, width), BF),
        scratch_shapes=[pltpu.VMEM((window * (2 if two else 1), LANES), F32)],
        cost_estimate=pl.CostEstimate(flops=0, bytes_accessed=rows * width * 12, transcendentals=0),
        name="unflatten",
    )(*blocks[a : a + 2 if two else a + 1])


def flatten(pos, b, mats, vecs, plan, core):
    part, span = plan.part, plan.rows
    shapes = []
    for off, mat in mats:
        lanes = mat.shape[1] // LANES
        shapes.append((off, mat.shape[0], lanes, round_up(-(-span // lanes) + 8, 8)))
    pad = round_up(max([w * c for _, _, c, w in shapes] + [v.shape[0] for _, v in vecs]), 8) + 8

    def first_row(t, pos_ref):
        return (8 * b + (pos_ref[1] ^ t) * 2 + (pos_ref[2] ^ core)) * span

    def start_row(p0, off, rows, lanes, w):
        return jnp.minimum(jnp.maximum(p0 - off, 0) // lanes // 8 * 8, rows - w)

    def kernel(pos_ref, *refs):
        ins = refs[: len(mats)]
        vins = refs[len(mats) : len(mats) + len(vecs)]
        out, wide = refs[len(mats) + len(vecs) :]
        p0 = first_row(pl.program_id(0), pos_ref)
        for (off, rows, lanes, w), ref in zip(shapes, ins):

            @pl.when((p0 + span > off) & (p0 < off + rows * lanes))
            def _():
                at = off + lanes * start_row(p0, off, rows, lanes, w) - p0 + pad
                for c in range(lanes):
                    wide[pl.ds(at + c, w, stride=lanes), :] = ref[:, c * LANES : (c + 1) * LANES]

        for (off, vec), ref in zip(vecs, vins):
            n = vec.shape[0]

            @pl.when((p0 + span > off) & (p0 < off + n))
            def _():
                at = off - p0 + pad
                for r in range(n):
                    wide[pl.ds(at + r, 1), :] = ref[r : r + 1, :]

        for k in range(4):
            at = pl.multiple_of(pad + (pos_ref[0] ^ k) * part, 8)
            out[k, 0] = wide[pl.ds(at, part), :].astype(BF)

    in_specs = [
        pl.BlockSpec(
            (pl.Element(w), pl.Element(lanes * LANES)),
            lambda t, p, off=off, rows=rows, lanes=lanes, w=w: (
                pl.multiple_of(start_row(first_row(t, p), off, rows, lanes, w), 8),
                0,
            ),
        )
        for off, rows, lanes, w in shapes
    ] + [pl.BlockSpec(v.shape, lambda t, p: (0, 0)) for _, v in vecs]
    shape = jax.ShapeDtypeStruct((4, 4, part, LANES), BF)
    return pl.pallas_call(
        kernel,
        grid_spec=pltpu.PrefetchScalarGridSpec(
            num_scalar_prefetch=1,
            grid=(4,),
            in_specs=in_specs,
            out_specs=pl.BlockSpec((4, 1, part, LANES), lambda t, p: (0, t, 0, 0)),
            scratch_shapes=[pltpu.VMEM((2 * pad + 4 * part, LANES), F32)],
        ),
        out_shape=shape,
        cost_estimate=pl.CostEstimate(flops=0, bytes_accessed=plan.block * LANES * 6, transcendentals=0),
        name="flatten",
    )(pos, *[m for _, m in mats], *[v for _, v in vecs])


class SumAll:
    def __init__(self, value):
        self.state = (value,)
        self.stage_number = 0

    def stage(self):
        total = sum(self.state)
        hops = ([(0, 1)], [(1, 0), (2, 0), (3, 0)], [(0, 2), (0, 4), (0, 6)], [])[self.stage_number]
        self.state = (total,) + tuple(send(total, *hop) for hop in hops)
        self.stage_number += 1


class Reduce:
    def __init__(self, half):
        self.state = (half(1), half(0))
        self.stage_number = 0

    def stage(self):
        self.exchange()
        self.stage_number += 1

    def exchange(self):
        s, now = self.stage_number, self.state
        wide = lambda *parts: sum(p.astype(F32) for p in parts)
        if s == 0:
            theirs, ours = now
            self.state = (ours, send(theirs, 0, 1))
        elif s == 1:
            ours = wide(*now).astype(BF)
            self.state = (ours, send(ours[3, :2], 1), send(ours[3, 2:], 2))
        elif s == 2:
            ours, by_x, by_y = now
            to_x = jnp.concatenate([ours[1, :2], wide(ours[1, 2:], by_y).astype(BF)])
            to_y = jnp.concatenate([wide(ours[2, :2], by_x).astype(BF), ours[2, 2:]])
            self.state = (ours[0], send(to_x, 1), send(to_y, 2))
        elif s == 3:
            line = wide(*now).astype(BF)
            self.state = (line[0],) + tuple(send(line[k], 0, 2 * k) for k in range(1, 4))
        else:
            self.state = wide(*now)


def advance(reduces, *values):
    states, values = tie([r.state for r in reduces], values)
    for r, state in zip(reduces, states):
        r.state = state
        r.stage()
    return values


def return_quarters(quarters, plan, pos):
    stack = jnp.stack(quarters)
    dp = pos[0]
    out = jnp.zeros_like(stack)
    for k in range(4):
        piece = pick(stack, dp ^ k)
        got = piece if k == 0 else send(piece, k)
        out = lax.dynamic_update_slice(out, got[None], (dp ^ k, 0, 0))
    return out.reshape(4 * plan.part, LANES)[: plan.rows].reshape(-1)


def segment_rows(d, ff):
    spans, at = [], 0
    for shape in segment_shapes(d, ff):
        length = math.prod(shape)
        spans.append((at, at + length, shape))
        at += length
    return spans, at


def cut(blocks, lo, hi):
    size = blocks[0].shape[0]
    pieces = []
    for i, block in enumerate(blocks):
        a, b = max(lo, i * size), min(hi, (i + 1) * size)
        if a < b:
            pieces.append(block[a - i * size : b - i * size])
    return pieces[0] if len(pieces) == 1 else jnp.concatenate(pieces)


def cut_padded(blocks, lo, hi, plan):
    pieces = []
    while lo < hi:
        end = min(hi, (lo // plan.rows + 1) * plan.rows)
        pieces.append(cut(blocks, plan.padded(lo), plan.padded(lo) + end - lo))
        lo = end
    return pieces[0] if len(pieces) == 1 else jnp.concatenate(pieces)


def matrix_of(blocks, lo, shape, plan):
    return unflatten(blocks, plan.padded(lo) // plan.block, lo, *shape, plan)


def stats(v):
    center = v - jnp.mean(v, axis=-1, keepdims=True)
    scale = lax.rsqrt(jnp.mean(center * center, axis=-1, keepdims=True) + EPS)
    return center * scale, scale


def norm_back(hat, scale, gain, grad):
    inner = grad * gain
    back = scale * (
        inner
        - jnp.mean(inner, axis=-1, keepdims=True)
        - hat * jnp.mean(inner * hat, axis=-1, keepdims=True)
    )
    return back, jnp.sum(grad * hat, axis=0), jnp.sum(grad, axis=0)


def product_back(grad_rows, weight):
    return lax.dot_general(grad_rows, weight, (((1,), (1,)), ((), ())), preferred_element_type=F32)


def row_sum(grad):
    return jnp.sum(grad.astype(F32), axis=0)


def gelu_pair(u):
    half = 0.5 * (1.0 + lax.erf(u * (2.0 ** -0.5)))
    slope = half + u * jnp.exp(-0.5 * u * u) * ((2.0 * math.pi) ** -0.5)
    return (u * half).astype(BF), slope


def bias_row(q_bias, v_bias):
    return jnp.concatenate([q_bias, jnp.zeros_like(q_bias), v_bias])


def layer(inputs, cotangent, params, clip_counts, slot_live):
    micro, clips, frames, places, d = inputs.shape
    n_sp = lax.axis_size("sp")
    n_dev = lax.axis_size("dp") * n_sp
    full_length = params.shape[0] * n_dev
    tokens = micro * clips * frames * places
    seqs = micro * clips * frames // n_sp
    length = places * n_sp
    rows = params.shape[0] // LANES
    fast = n_sp == 8 and n_dev == 32 and params.shape[0] % (2 * LANES) == 0
    spans, used = segment_rows(d, FF)
    inputs_now, cot_now, live_now = inputs, cotangent, slot_live

    if fast:
        plan, pos = Plan(rows), place_of()
        blocks = [None] * 4
        made = {}

        def piece(i):
            if i not in made:
                lo, hi, shape = spans[i]
                if len(shape) == 1:
                    made[i] = cut_padded(blocks, lo // LANES, hi // LANES, plan).reshape(shape).astype(F32)
                else:
                    made[i] = matrix_of(blocks, lo // LANES, shape, plan)
            return made[i]

        gather = Gather(params, plan, pos)
        gather.stage()
        inputs_now, cot_now, live_now = gather.sync(inputs_now, cot_now, live_now)
    else:
        flat = lax.all_gather(params, BOTH, axis=0, tiled=True).reshape(-1, LANES)

        def piece(i):
            lo, hi, shape = spans[i]
            got = flat[lo // LANES : hi // LANES].reshape(shape)
            return got.astype(F32) if len(shape) == 1 else got

    in_use = (jnp.arange(clips, dtype=jnp.int32)[None] < clip_counts).astype(F32)
    live = live_now.astype(F32) * in_use[:, :, None]
    live_low = live.astype(BF)[:, :, None, :, None]

    def to_frames(value):
        return lax.all_to_all(
            value.reshape(micro, clips * frames, places, d), "sp", split_axis=1, concat_axis=2, tiled=True
        ).reshape(seqs * length, d)

    def to_places(value):
        return lax.all_to_all(
            value.reshape(micro, seqs // micro, length, d), "sp", split_axis=2, concat_axis=1, tiled=True
        ).reshape(micro, clips, frames, places, d)

    x_low = inputs_now.reshape(tokens, d)
    masked = (cot_now * live_low).reshape(micro, clips * frames, places, d)
    live_sent = jnp.broadcast_to(live.astype(BF)[:, :, None], (micro, clips, frames, places)).reshape(
        micro, clips * frames, places
    )
    if fast:
        gather.stage()
        x_low, live_sent = gather.sync(x_low, live_sent)
    x = x_low.astype(F32)
    hat1, scale1 = stats(x)
    live_frames = lax.all_to_all(live_sent, "sp", split_axis=1, concat_axis=2, tiled=True)
    keep_rows = live_frames.astype(F32).reshape(seqs, 1, length)
    keep_s = keep_rows.reshape(seqs, length, 1)

    span_t = frames * places
    place = jnp.arange(span_t, dtype=jnp.int32) % places
    same = (place[:, None] == place[None]).astype(F32)[None]

    if fast:
        gather.stage()
        hat1, scale1 = gather.sync(hat1, scale1)
        gather.stage()
        blocks[0] = gather.block(0)
        made[2] = piece(2)
        made[2], masked = gather.sync(made[2], masked)
        gather.stage()

    dx3 = to_frames(masked)
    tg = piece(0)
    h1 = (hat1 * tg + piece(1)).astype(BF)
    w_qkv_t = piece(2)
    qkv_t = (dot(h1, w_qkv_t) + bias_row(piece(3), piece(4))).astype(BF)
    qkv_t = qkv_t.reshape(micro * clips, span_t, 3 * d)
    o_t = attend(qkv_t, same, d).reshape(tokens, d)
    if fast:
        (o_t,) = gather.sync(o_t)
        gather.stage()
    w_out_t = piece(5)
    a_t = (dot(o_t, w_out_t) + piece(6)).astype(BF)
    if fast:
        (a_t,) = gather.sync(a_t)
        blocks[1] = gather.block(1)
        gather.stage()
    w_fc = piece(7)
    x1 = (x + dot(a_t, w_fc) + piece(8)).astype(BF)
    if fast:
        x1, dx3 = gather.sync(x1, dx3)
        gather.stage()
    xb = to_frames(x1)
    if fast:
        blocks[2], blocks[3] = gather.block(2), gather.block(3)

    w_qkv_s, w_out_s, w_up, w_down = piece(11), piece(14), piece(18), piece(20)
    if fast:
        xb, w_qkv_s, w_out_s, w_up, w_down = tie(xb, w_qkv_s, w_out_s, w_up, w_down)
    xb = xb.astype(F32)
    hat2, scale2 = stats(xb)
    sg = piece(9)
    h2 = (hat2 * sg + piece(10)).astype(BF)
    qkv_s = (dot(h2, w_qkv_s) + bias_row(piece(12), piece(13))).astype(BF)
    qkv_s = qkv_s.reshape(seqs, length, 3 * d)
    o_s = attend(qkv_s, keep_rows, d).reshape(-1, d)
    x2 = xb + dot(o_s, w_out_s) + piece(15)
    hat3, scale3 = stats(x2)
    mg = piece(16)
    h3 = (hat3 * mg + piece(17)).astype(BF)
    g, slope = gelu_pair(dot(h3, w_up) + piece(19))
    x3 = (x2 + dot(g, w_down) + piece(21)).astype(BF)
    out = to_places(x3)

    du = (product_back(dx3, w_down) * slope).astype(BF)
    back3, grad_mg, grad_mb = norm_back(hat3, scale3, mg, product_back(du, w_up))
    dx2 = dx3.astype(F32) + back3
    da_s = dx2.astype(BF)
    do_s = product_back(da_s, w_out_s).astype(BF)
    dqkv_s = attend_back(qkv_s, keep_s, do_s.reshape(seqs, length, d), d).reshape(-1, 3 * d)
    back2, grad_sg, grad_sb = norm_back(hat2, scale2, sg, product_back(dqkv_s, w_qkv_s))
    dx1 = to_places((dx2 + back2).astype(BF)).reshape(tokens, d)

    grads = [None] * len(spans)
    grads[20], grads[21] = dot_l(g, dx3), row_sum(dx3)
    grads[18], grads[19] = dot_l(h3, du), row_sum(du)
    grads[14], grads[15] = dot_l(o_s, da_s), row_sum(da_s)
    grads[16], grads[17] = grad_mg, grad_mb
    grads[9], grads[10] = grad_sg, grad_sb

    def block_of(b):
        size = 8 * rows
        tail = jnp.zeros((full_length - used,), F32)
        mats, vecs, run, run_at = [], [], [], 0
        for i, (lo, hi, shape) in enumerate(spans + [(used, full_length, (full_length - used,))]):
            inside = lo < (b + 1) * size * LANES and hi > b * size * LANES
            if len(shape) == 2 or not inside:
                if run:
                    vecs.append((run_at, jnp.concatenate(run).reshape(-1, LANES)))
                run = []
                if inside:
                    mats.append((lo // LANES, grads[i]))
            else:
                run_at = run_at if run else lo // LANES
                run.append(grads[i] if i < len(grads) else tail)
        if run:
            vecs.append((run_at, jnp.concatenate(run).reshape(-1, LANES)))

        def half(core):
            return flatten(pos, b, mats, vecs, plan, core)

        return Reduce(half)

    if fast:
        r3 = block_of(3)
        r3.stage()
        r2 = block_of(2)
        r2.stage()
    grads[11] = dot_l(h2, dqkv_s)
    sums = row_sum(dqkv_s)
    grads[12], grads[13] = sums[:d], sums[2 * d :]
    if fast:
        dx1, grads[11] = advance((r3, r2), dx1, grads[11])

    da_t = product_back(dx1, w_fc).astype(BF)
    do_t = product_back(da_t, w_out_t).astype(BF)
    grads[7], grads[8] = dot_l(a_t, dx1), row_sum(dx1)
    if fast:
        do_t, grads[7] = advance((r3, r2), do_t, grads[7])
        r1 = block_of(1)
        r1.stage()
    dqkv_t = attend_back(qkv_t, same, do_t.reshape(micro * clips, span_t, d), d).reshape(tokens, 3 * d)
    if fast:
        (dqkv_t,) = advance((r3, r2, r1), dqkv_t)
    sums = row_sum(dqkv_t)
    grads[3], grads[4] = sums[:d], sums[2 * d :]
    grads[5], grads[6] = dot_l(o_t, da_t), row_sum(da_t)
    grads[2] = dot_l(h1, dqkv_t)
    if fast:
        grads[2], dqkv_t, out = advance((r3, r2, r1), grads[2], dqkv_t, out)
        grads[0] = grads[1] = jnp.zeros((d,), F32)
        r0 = block_of(0)
        r0.stage()
    back1, grad_tg, grad_tb = norm_back(hat1, scale1, tg, product_back(dqkv_t, w_qkv_t))
    if fast:
        norm_sum = SumAll(jnp.concatenate([grad_tg, grad_tb]).reshape(-1, LANES))
        norm_sum.stage()
        back1, out = advance((r1, r0, norm_sum), back1, out)
        (back1,) = advance((r1, r0, norm_sum), back1)
    else:
        grads[0], grads[1] = grad_tg, grad_tb
    out = out * live_low
    input_grad = (dx1.astype(F32) + back1).astype(BF).reshape(inputs.shape)

    if fast:
        advance((r0, norm_sum))
        advance((r0,))
        first = (pos[0] + pos[1] + pos[2] == 0).astype(F32)
        extra = norm_sum.state[0] * first
        extra = jnp.pad(extra, ((0, plan.part - extra.shape[0]), (0, 0)))
        param_grad = return_quarters([r0.state + extra, r1.state, r2.state, r3.state], plan, pos)
    else:
        flat = jnp.concatenate([g.reshape(-1) for g in grads] + [jnp.zeros((full_length - used,), F32)])
        param_grad = lax.psum_scatter(flat, BOTH, scatter_dimension=0, tiled=True)
    return (out, input_grad, param_grad)


def solution(mesh):
    tokens = P(None, "dp", None, "sp", None)
    return jax.shard_map(
        layer,
        mesh=mesh,
        in_specs=(tokens, tokens, P(BOTH), P(None, "dp"), P(None, "dp", "sp")),
        out_specs=(tokens, tokens, P(BOTH)),
        check_vma=False,
    )
```

```python
import math

import jax
import jax.numpy as jnp
from jax import lax
from jax.experimental import pallas as pl
from jax.experimental.pallas import tpu as pltpu
from jax.sharding import PartitionSpec as P


FF = 3072
EPS = 1e-06
MASKED = -1000000000.0
LANES = 128
BOTH = ("dp", "sp")
BF = jnp.bfloat16
F32 = jnp.float32


def segment_shapes(d, ff):
    return [
        (d,), (d,), (d, 3 * d), (d,), (d,), (d, d), (d,), (d, d), (d,),
        (d,), (d,), (d, 3 * d), (d,), (d,), (d, d), (d,),
        (d,), (d,), (d, ff), (ff,), (ff, d), (d,),
    ]


def pair_masks(rows):
    lane = lax.broadcasted_iota(jnp.int32, (rows, LANES), 1)
    return lane < LANES // 2


def dot_l(a, b):
    return lax.dot_general(a, b, (((0,), (0,)), ((), ())), preferred_element_type=F32)


def dot(a, b):
    return jnp.dot(a, b, preferred_element_type=F32)


def turn(t):
    return jnp.transpose(t.astype(F32)).astype(BF)


def halves(t):
    half = LANES // 2
    zero = jnp.zeros_like(t[:half])
    return jnp.concatenate([t[:half], zero]), jnp.concatenate([zero, t[half:]])


def exp_of(k, q_turned, keep):
    s = jnp.where(keep, dot(k, q_turned), MASKED)
    e = jnp.exp(s - jnp.max(s, axis=0, keepdims=True))
    return e, 1.0 / jnp.sum(e, axis=0, keepdims=True)


def softmax_of(q, k, keep):
    s = lax.dot_general(q, k, (((1,), (1,)), ((), ())), preferred_element_type=F32)
    s = jnp.where(keep, s, MASKED)
    e = jnp.exp(s - jnp.max(s, axis=-1, keepdims=True))
    return e.astype(BF), 1.0 / jnp.sum(e, axis=-1, keepdims=True)


def attend_kernel(q_ref, k_ref, v_ref, m_ref, o_ref):
    rows, width = q_ref.shape[1], q_ref.shape[2]
    keep = m_ref[0] > 0.5
    first = pair_masks(rows)
    for at in range(0, width, LANES):
        q = q_ref[0, :, at : at + LANES] * jnp.asarray(0.125, BF)
        k = k_ref[0, :, at : at + LANES]
        v = v_ref[0, :, at : at + LANES]
        zero = jnp.zeros_like(q)
        ea, scale_a = softmax_of(jnp.where(first, q, zero), k, keep)
        eb, scale_b = softmax_of(jnp.where(first, zero, q), k, keep)
        o_ref[0, :, at : at + LANES] = jnp.where(first, dot(ea, v) * scale_a, dot(eb, v) * scale_b).astype(BF)


def attend_back_kernel(q_ref, k_ref, v_ref, m_ref, d_ref, o_ref):
    rows, width = q_ref.shape[1], q_ref.shape[2]
    d_model = o_ref.shape[2] // 3
    keep = jnp.broadcast_to(m_ref[0], (rows, rows)) > 0.5
    half = LANES // 2
    first = pair_masks(rows)
    for at in range(0, width, LANES):
        q = q_ref[0, :, at : at + LANES] * jnp.asarray(0.125, BF)
        k = k_ref[0, :, at : at + LANES]
        v = v_ref[0, :, at : at + LANES]
        d = d_ref[0, :, at : at + LANES]
        k_turned = turn(k)
        qs, ds_ = halves(turn(q)), halves(turn(d))
        dqs, dks, dvs = [], [], []
        for head in range(2):
            e, scale = exp_of(k, qs[head], keep)
            p = e * scale
            dp = dot(v, ds_[head])
            ds = (p * (dp - jnp.sum(p * dp, axis=0, keepdims=True))).astype(BF)
            dqs.append(dot(k_turned[head * half : (head + 1) * half], ds))
            dks.append(dot(ds, q))
            dvs.append(dot(p.astype(BF), d))
        results = (
            jnp.transpose(jnp.concatenate(dqs) * 0.125),
            jnp.where(first, *dks),
            jnp.where(first, *dvs),
        )
        for third, result in enumerate(results):
            to = pl.multiple_of(third * d_model + pl.program_id(1) * width + at, LANES)
            o_ref[0, :, pl.ds(to, LANES)] = result.astype(BF)


def head_split(width):
    for parts in (2, 3, 1):
        if width % (parts * LANES) == 0:
            return parts
    return 1


def attention_specs(packed, keep, d):
    parts = head_split(d)
    w = d // parts
    rows = packed.shape[1]
    own = lambda third: pl.BlockSpec((1, rows, w), lambda i, j: (i, 0, third * parts + j))
    one = keep.shape[0] == 1
    mask = pl.BlockSpec((1,) + keep.shape[1:], lambda i, j: (0 if one else i, 0, 0))
    flat = pl.BlockSpec((1, rows, w), lambda i, j: (i, 0, j))
    return parts, own, mask, flat


def attend(packed, keep, d):
    n, rows, _ = packed.shape
    parts, own, mask, flat = attention_specs(packed, keep, d)
    return pl.pallas_call(
        attend_kernel,
        grid=(n, parts),
        in_specs=[own(0), own(1), own(2), mask],
        out_specs=flat,
        out_shape=jax.ShapeDtypeStruct((n, rows, d), BF),
        cost_estimate=pl.CostEstimate(
            flops=4 * n * rows * rows * d * 2,
            bytes_accessed=n * rows * d * 8,
            transcendentals=n * rows * rows * (d // 64),
        ),
        name="attend",
    )(packed, packed, packed, keep)


def attend_back(packed, keep, grad, d):
    n, rows, _ = packed.shape
    parts, own, mask, flat = attention_specs(packed, keep, d)
    return pl.pallas_call(
        attend_back_kernel,
        grid=(n, parts),
        in_specs=[own(0), own(1), own(2), mask, flat],
        out_specs=pl.BlockSpec((1, rows, 3 * d), lambda i, j: (i, 0, 0)),
        out_shape=jax.ShapeDtypeStruct((n, rows, 3 * d), BF),
        cost_estimate=pl.CostEstimate(
            flops=10 * n * rows * rows * d * 2,
            bytes_accessed=n * rows * d * 14,
            transcendentals=n * rows * rows * (d // 64),
        ),
        name="attend_back",
    )(packed, packed, packed, keep, grad)


def flip_perm(dp_bits=0, sp_bits=0):
    return [(d * 8 + s, (d ^ dp_bits) * 8 + (s ^ sp_bits)) for d in range(4) for s in range(8)]


def send(value, dp_bits=0, sp_bits=0):
    return lax.ppermute(value, BOTH, flip_perm(dp_bits, sp_bits))


def pick(stack, at):
    return lax.dynamic_index_in_dim(stack, at, 0, keepdims=False)


def place_of():
    dp, sp = lax.axis_index("dp"), lax.axis_index("sp")
    return jnp.stack([dp, sp >> 1, sp & 1]).astype(jnp.int32)


def round_up(value, step):
    return -(-value // step) * step


class Plan:
    def __init__(self, rows):
        self.rows = rows
        self.part = round_up(-(-rows // 4), 16)
        self.gap = 4 * self.part - rows
        self.block = 32 * self.part

    def padded(self, row):
        return row + self.gap * (row // self.rows)


def assemble_kernel(pos_ref, *refs):
    ins, out, buf, sem_in, sem_out = refs[:8], refs[8], refs[9], refs[10], refs[11]
    dp, z, core = pos_ref[0], pos_ref[1], pos_ref[2]
    loads = []
    for j in range(8):
        for k in range(4):
            at = j * 4 + k
            load = pltpu.make_async_copy(ins[j].at[k], buf.at[at], sem_in.at[at])
            load.start()
            loads.append(load)
    stores = []
    for j in range(8):
        for k in range(4):
            at = j * 4 + k
            loads[at].wait()
            to = ((z ^ k) * 2 + (core ^ (j // 4))) * 4 + (dp ^ (j % 4))
            store = pltpu.make_async_copy(buf.at[at], out.at[to], sem_out.at[at])
            store.start()
            stores.append(store)
    for store in stores:
        store.wait()


def assemble(pos, pieces):
    part = pieces[0].shape[1]
    any_spec = pl.BlockSpec(memory_space=pl.ANY)
    out = pl.pallas_call(
        assemble_kernel,
        grid_spec=pltpu.PrefetchScalarGridSpec(
            num_scalar_prefetch=1,
            grid=(1,),
            in_specs=[any_spec] * 8,
            out_specs=any_spec,
            scratch_shapes=[
                pltpu.VMEM((32, part, LANES), BF),
                pltpu.SemaphoreType.DMA((32,)),
                pltpu.SemaphoreType.DMA((32,)),
            ],
        ),
        out_shape=jax.ShapeDtypeStruct((32, part, LANES), BF),
        cost_estimate=pl.CostEstimate(flops=0, bytes_accessed=32 * part * LANES * 4, transcendentals=0),
        name="assemble",
    )(pos, *pieces)
    return out.reshape(32 * part, LANES)


def tie(*values):
    return lax.optimization_barrier(values)


class Gather:
    SCHEDULE = (
        ((0, 0),),
        ((0, 1), (1, 0)),
        ((0, 2), (2, 0)),
        ((0, 3), (1, 1), (3, 0)),
        ((1, 2), (2, 1)),
        ((1, 3), (2, 2), (3, 1)),
        ((2, 3), (3, 2)),
        ((3, 3),),
    )

    def __init__(self, shard, plan, pos):
        self.plan, self.pos = plan, pos
        dp = pos[0]
        mine = jnp.pad(shard.reshape(plan.rows, LANES), ((0, plan.gap), (0, 0)))
        mine = mine.reshape(4, plan.part, LANES)
        spread = jnp.zeros_like(mine)
        for k in range(4):
            piece = pick(mine, dp ^ k)
            got = piece if k == 0 else send(piece, k)
            spread = lax.dynamic_update_slice(spread, got[None], (dp ^ k, 0, 0))
        self.state = [[spread[b]] for b in range(4)]
        self.stage_number = 0

    def stage(self):
        self.exchange()
        self.stage_number += 1

    def exchange(self):
        for b, step in self.SCHEDULE[self.stage_number]:
            now = self.state[b]
            if step == 0:
                now = now + [send(now[0], 0, 2 * k) for k in range(1, 4)]
            elif step == 1:
                line = jnp.stack(now)
                now = [line, send(line, 1), send(line, 2)]
            elif step == 2:
                line, by_x, by_y = now
                now = [line, by_x, by_y, jnp.concatenate([send(by_x[:2], 2), send(by_y[2:], 1)])]
            else:
                now = now + [send(part, 0, 1) for part in now]
            self.state[b] = now

    def sync(self, *values):
        self.state, values = tie(self.state, values)
        return values

    def block(self, b):
        return assemble(self.pos, self.state[b])


CHUNK = 1152


def unflatten(blocks, a, off, rows, width, plan):
    lanes = width // LANES
    step_rows = CHUNK // lanes
    size = plan.block
    window = round_up(CHUNK + plan.gap + 16, 16)
    two = plan.padded(off + rows * lanes - 1) >= (a + 1) * size

    def where_from(i):
        first = off + CHUNK * i
        at = first + plan.gap * (first // plan.rows) - a * size
        start = jnp.minimum(at // 16 * 16, size - window)
        start_next = jnp.clip((at - size) // 16 * 16, 0, size - window)
        return first, at, start, start_next

    def kernel(*refs):
        in_ref, out_ref, wide = refs[0], refs[-2], refs[-1]
        first, at, start, start_next = where_from(pl.program_id(0))
        left = plan.rows - first % plan.rows
        delta = at - start
        over = delta + plan.gap
        if two:
            delta = jnp.where(at < size, delta, at - size - start_next)
            crossing = (at < size) & (at + left + plan.gap >= size)
            over = jnp.where(crossing, window - left, delta + plan.gap)

            @pl.when(at < size)
            def _():
                wide[:window] = in_ref[...].astype(F32)

            @pl.when(at >= size)
            def _():
                wide[:window] = refs[1][...].astype(F32)

            @pl.when(crossing)
            def _():
                wide[window:] = refs[1][...].astype(F32)

        else:
            wide[:window] = in_ref[...].astype(F32)

        @pl.when(left >= CHUNK)
        def _():
            for b in range(lanes):
                got = wide[pl.ds(delta + b, step_rows, stride=lanes), :]
                out_ref[:, b * LANES : (b + 1) * LANES] = got.astype(BF)

        @pl.when(left < CHUNK)
        def _():
            row = lax.broadcasted_iota(jnp.int32, (step_rows, LANES), 0) * lanes
            for b in range(lanes):
                near = wide[pl.ds(delta + b, step_rows, stride=lanes), :]
                far = wide[pl.ds(over + b, step_rows, stride=lanes), :]
                got = jnp.where(row + b < left, near, far)
                out_ref[:, b * LANES : (b + 1) * LANES] = got.astype(BF)

    element = (pl.Element(window), pl.Element(LANES))
    in_specs = [pl.BlockSpec(element, lambda i: (pl.multiple_of(where_from(i)[2], 16), 0))]
    if two:
        in_specs.append(pl.BlockSpec(element, lambda i: (pl.multiple_of(where_from(i)[3], 16), 0)))
    return pl.pallas_call(
        kernel,
        grid=(rows // step_rows,),
        in_specs=in_specs,
        out_specs=pl.BlockSpec((step_rows, width), lambda i: (i, 0)),
        out_shape=jax.ShapeDtypeStruct((rows, width), BF),
        scratch_shapes=[pltpu.VMEM((window * (2 if two else 1), LANES), F32)],
        cost_estimate=pl.CostEstimate(flops=0, bytes_accessed=rows * width * 12, transcendentals=0),
        name="unflatten",
    )(*blocks[a : a + 2 if two else a + 1])


def flatten(pos, b, mats, vecs, plan, core):
    part, span = plan.part, plan.rows
    shapes = []
    for off, mat in mats:
        lanes = mat.shape[1] // LANES
        shapes.append((off, mat.shape[0], lanes, round_up(-(-span // lanes) + 8, 8)))
    pad = round_up(max([w * c for _, _, c, w in shapes] + [v.shape[0] for _, v in vecs]), 8) + 8

    def first_row(t, pos_ref):
        return (8 * b + (pos_ref[1] ^ t) * 2 + (pos_ref[2] ^ core)) * span

    def start_row(p0, off, rows, lanes, w):
        return jnp.minimum(jnp.maximum(p0 - off, 0) // lanes // 8 * 8, rows - w)

    def kernel(pos_ref, *refs):
        ins = refs[: len(mats)]
        vins = refs[len(mats) : len(mats) + len(vecs)]
        out, wide = refs[len(mats) + len(vecs) :]
        p0 = first_row(pl.program_id(0), pos_ref)
        for (off, rows, lanes, w), ref in zip(shapes, ins):

            @pl.when((p0 + span > off) & (p0 < off + rows * lanes))
            def _():
                at = off + lanes * start_row(p0, off, rows, lanes, w) - p0 + pad
                for c in range(lanes):
                    wide[pl.ds(at + c, w, stride=lanes), :] = ref[:, c * LANES : (c + 1) * LANES]

        for (off, vec), ref in zip(vecs, vins):
            n = vec.shape[0]

            @pl.when((p0 + span > off) & (p0 < off + n))
            def _():
                at = off - p0 + pad
                for r in range(n):
                    wide[pl.ds(at + r, 1), :] = ref[r : r + 1, :]

        for k in range(4):
            at = pl.multiple_of(pad + (pos_ref[0] ^ k) * part, 8)
            out[k, 0] = wide[pl.ds(at, part), :].astype(BF)

    in_specs = [
        pl.BlockSpec(
            (pl.Element(w), pl.Element(lanes * LANES)),
            lambda t, p, off=off, rows=rows, lanes=lanes, w=w: (
                pl.multiple_of(start_row(first_row(t, p), off, rows, lanes, w), 8),
                0,
            ),
        )
        for off, rows, lanes, w in shapes
    ] + [pl.BlockSpec(v.shape, lambda t, p: (0, 0)) for _, v in vecs]
    shape = jax.ShapeDtypeStruct((4, 4, part, LANES), BF)
    return pl.pallas_call(
        kernel,
        grid_spec=pltpu.PrefetchScalarGridSpec(
            num_scalar_prefetch=1,
            grid=(4,),
            in_specs=in_specs,
            out_specs=pl.BlockSpec((4, 1, part, LANES), lambda t, p: (0, t, 0, 0)),
            scratch_shapes=[pltpu.VMEM((2 * pad + 4 * part, LANES), F32)],
        ),
        out_shape=shape,
        cost_estimate=pl.CostEstimate(flops=0, bytes_accessed=plan.block * LANES * 6, transcendentals=0),
        name="flatten",
    )(pos, *[m for _, m in mats], *[v for _, v in vecs])


class SumAll:
    def __init__(self, value):
        self.state = (value,)
        self.stage_number = 0

    def stage(self):
        total = sum(self.state)
        hops = ([(0, 1)], [(1, 0), (2, 0), (3, 0)], [(0, 2), (0, 4), (0, 6)], [])[self.stage_number]
        self.state = (total,) + tuple(send(total, *hop) for hop in hops)
        self.stage_number += 1


class Reduce:
    def __init__(self, half):
        self.state = (half(1), half(0))
        self.stage_number = 0

    def stage(self):
        self.exchange()
        self.stage_number += 1

    def exchange(self):
        s, now = self.stage_number, self.state
        wide = lambda *parts: sum(p.astype(F32) for p in parts)
        if s == 0:
            theirs, ours = now
            self.state = (ours, send(theirs, 0, 1))
        elif s == 1:
            ours = wide(*now).astype(BF)
            self.state = (ours, send(ours[3, :2], 1), send(ours[3, 2:], 2))
        elif s == 2:
            ours, by_x, by_y = now
            to_x = jnp.concatenate([ours[1, :2], wide(ours[1, 2:], by_y).astype(BF)])
            to_y = jnp.concatenate([wide(ours[2, :2], by_x).astype(BF), ours[2, 2:]])
            self.state = (ours[0], send(to_x, 1), send(to_y, 2))
        elif s == 3:
            line = wide(*now).astype(BF)
            self.state = (line[0],) + tuple(send(line[k], 0, 2 * k) for k in range(1, 4))
        else:
            self.state = wide(*now)


def advance(reduces, *values):
    states, values = tie([r.state for r in reduces], values)
    for r, state in zip(reduces, states):
        r.state = state
        r.stage()
    return values


def return_quarters(quarters, plan, pos):
    stack = jnp.stack(quarters)
    dp = pos[0]
    out = jnp.zeros_like(stack)
    for k in range(4):
        piece = pick(stack, dp ^ k)
        got = piece if k == 0 else send(piece, k)
        out = lax.dynamic_update_slice(out, got[None], (dp ^ k, 0, 0))
    return out.reshape(4 * plan.part, LANES)[: plan.rows].reshape(-1)


def segment_rows(d, ff):
    spans, at = [], 0
    for shape in segment_shapes(d, ff):
        length = math.prod(shape)
        spans.append((at, at + length, shape))
        at += length
    return spans, at


def cut(blocks, lo, hi):
    size = blocks[0].shape[0]
    pieces = []
    for i, block in enumerate(blocks):
        a, b = max(lo, i * size), min(hi, (i + 1) * size)
        if a < b:
            pieces.append(block[a - i * size : b - i * size])
    return pieces[0] if len(pieces) == 1 else jnp.concatenate(pieces)


def cut_padded(blocks, lo, hi, plan):
    pieces = []
    while lo < hi:
        end = min(hi, (lo // plan.rows + 1) * plan.rows)
        pieces.append(cut(blocks, plan.padded(lo), plan.padded(lo) + end - lo))
        lo = end
    return pieces[0] if len(pieces) == 1 else jnp.concatenate(pieces)


def matrix_of(blocks, lo, shape, plan):
    return unflatten(blocks, plan.padded(lo) // plan.block, lo, *shape, plan)


def stats(v):
    center = v - jnp.mean(v, axis=-1, keepdims=True)
    scale = lax.rsqrt(jnp.mean(center * center, axis=-1, keepdims=True) + EPS)
    return center * scale, scale


def norm_back(hat, scale, gain, grad):
    inner = grad * gain
    back = scale * (
        inner
        - jnp.mean(inner, axis=-1, keepdims=True)
        - hat * jnp.mean(inner * hat, axis=-1, keepdims=True)
    )
    return back, jnp.sum(grad * hat, axis=0), jnp.sum(grad, axis=0)


def product_back(grad_rows, weight):
    return lax.dot_general(grad_rows, weight, (((1,), (1,)), ((), ())), preferred_element_type=F32)


def row_sum(grad):
    return jnp.sum(grad.astype(F32), axis=0)


def gelu_pair(u):
    half = 0.5 * (1.0 + lax.erf(u * (2.0 ** -0.5)))
    slope = half + u * jnp.exp(-0.5 * u * u) * ((2.0 * math.pi) ** -0.5)
    return (u * half).astype(BF), slope


def bias_row(q_bias, v_bias):
    return jnp.concatenate([q_bias, jnp.zeros_like(q_bias), v_bias])


def layer(inputs, cotangent, params, clip_counts, slot_live):
    micro, clips, frames, places, d = inputs.shape
    n_sp = lax.axis_size("sp")
    n_dev = lax.axis_size("dp") * n_sp
    full_length = params.shape[0] * n_dev
    tokens = micro * clips * frames * places
    seqs = micro * clips * frames // n_sp
    length = places * n_sp
    rows = params.shape[0] // LANES
    fast = n_sp == 8 and n_dev == 32 and params.shape[0] % (2 * LANES) == 0
    spans, used = segment_rows(d, FF)
    inputs_now, cot_now, live_now = inputs, cotangent, slot_live

    if fast:
        plan, pos = Plan(rows), place_of()
        blocks = [None] * 4
        made = {}

        def piece(i):
            if i not in made:
                lo, hi, shape = spans[i]
                if len(shape) == 1:
                    made[i] = cut_padded(blocks, lo // LANES, hi // LANES, plan).reshape(shape).astype(F32)
                else:
                    made[i] = matrix_of(blocks, lo // LANES, shape, plan)
            return made[i]

        gather = Gather(params, plan, pos)
        gather.stage()
        inputs_now, cot_now, live_now = gather.sync(inputs_now, cot_now, live_now)
    else:
        flat = lax.all_gather(params, BOTH, axis=0, tiled=True).reshape(-1, LANES)

        def piece(i):
            lo, hi, shape = spans[i]
            got = flat[lo // LANES : hi // LANES].reshape(shape)
            return got.astype(F32) if len(shape) == 1 else got

    in_use = (jnp.arange(clips, dtype=jnp.int32)[None] < clip_counts).astype(F32)
    live = live_now.astype(F32) * in_use[:, :, None]
    live_low = live.astype(BF)[:, :, None, :, None]

    def to_frames(value):
        return lax.all_to_all(
            value.reshape(micro, clips * frames, places, d), "sp", split_axis=1, concat_axis=2, tiled=True
        ).reshape(seqs * length, d)

    def to_places(value):
        return lax.all_to_all(
            value.reshape(micro, seqs // micro, length, d), "sp", split_axis=2, concat_axis=1, tiled=True
        )

    x_low = inputs_now.reshape(tokens, d)
    masked = (cot_now * live_low).reshape(micro, clips * frames, places, d)
    live_sent = jnp.broadcast_to(live.astype(BF)[:, :, None], (micro, clips, frames, places)).reshape(
        micro, clips * frames, places
    )
    if fast:
        gather.stage()
        x_low, live_sent = gather.sync(x_low, live_sent)
    x = x_low.astype(F32)
    hat1, scale1 = stats(x)
    live_frames = lax.all_to_all(live_sent, "sp", split_axis=1, concat_axis=2, tiled=True)
    keep_rows = live_frames.astype(F32).reshape(seqs, 1, length)
    keep_s = keep_rows.reshape(seqs, length, 1)

    span_t = frames * places
    place = jnp.arange(span_t, dtype=jnp.int32) % places
    same = (place[:, None] == place[None]).astype(F32)[None]

    if fast:
        gather.stage()
        hat1, scale1 = gather.sync(hat1, scale1)
        gather.stage()
        blocks[0] = gather.block(0)
        made[2] = piece(2)
        made[2], masked = gather.sync(made[2], masked)
        gather.stage()

    dx3 = to_frames(masked)
    tg = piece(0)
    h1 = (hat1 * tg + piece(1)).astype(BF)
    w_qkv_t = piece(2)
    qkv_t = (dot(h1, w_qkv_t) + bias_row(piece(3), piece(4))).astype(BF)
    qkv_t = qkv_t.reshape(micro * clips, span_t, 3 * d)
    o_t = attend(qkv_t, same, d).reshape(tokens, d)
    if fast:
        (o_t,) = gather.sync(o_t)
        gather.stage()
    w_out_t = piece(5)
    a_t = (dot(o_t, w_out_t) + piece(6)).astype(BF)
    if fast:
        (a_t,) = gather.sync(a_t)
        blocks[1] = gather.block(1)
        gather.stage()
    w_fc = piece(7)
    x1 = (x + dot(a_t, w_fc) + piece(8)).astype(BF)
    if fast:
        x1, dx3 = gather.sync(x1, dx3)
        gather.stage()
    xb = to_frames(x1)
    if fast:
        blocks[2], blocks[3] = gather.block(2), gather.block(3)

    w_qkv_s, w_out_s, w_up, w_down = piece(11), piece(14), piece(18), piece(20)
    if fast:
        xb, w_qkv_s, w_out_s, w_up, w_down = tie(xb, w_qkv_s, w_out_s, w_up, w_down)
    xb = xb.astype(F32)
    hat2, scale2 = stats(xb)
    sg = piece(9)
    h2 = (hat2 * sg + piece(10)).astype(BF)
    qkv_s = (dot(h2, w_qkv_s) + bias_row(piece(12), piece(13))).astype(BF)
    qkv_s = qkv_s.reshape(seqs, length, 3 * d)
    o_s = attend(qkv_s, keep_rows, d).reshape(-1, d)
    x2 = xb + dot(o_s, w_out_s) + piece(15)
    hat3, scale3 = stats(x2)
    mg = piece(16)
    h3 = (hat3 * mg + piece(17)).astype(BF)
    g, slope = gelu_pair(dot(h3, w_up) + piece(19))
    x3 = (x2 + dot(g, w_down) + piece(21)).astype(BF)
    out = to_places(x3)

    du = (product_back(dx3, w_down) * slope).astype(BF)
    back3, grad_mg, grad_mb = norm_back(hat3, scale3, mg, product_back(du, w_up))
    dx2 = dx3.astype(F32) + back3
    da_s = dx2.astype(BF)
    do_s = product_back(da_s, w_out_s).astype(BF)
    dqkv_s = attend_back(qkv_s, keep_s, do_s.reshape(seqs, length, d), d).reshape(-1, 3 * d)
    back2, grad_sg, grad_sb = norm_back(hat2, scale2, sg, product_back(dqkv_s, w_qkv_s))
    dx1 = to_places((dx2 + back2).astype(BF)).reshape(tokens, d)

    grads = [None] * len(spans)
    grads[20], grads[21] = dot_l(g, dx3), row_sum(dx3)
    grads[18], grads[19] = dot_l(h3, du), row_sum(du)
    grads[14], grads[15] = dot_l(o_s, da_s), row_sum(da_s)
    grads[16], grads[17] = grad_mg, grad_mb
    grads[9], grads[10] = grad_sg, grad_sb

    def block_of(b):
        size = 8 * rows
        tail = jnp.zeros((full_length - used,), F32)
        mats, vecs, run, run_at = [], [], [], 0
        for i, (lo, hi, shape) in enumerate(spans + [(used, full_length, (full_length - used,))]):
            inside = lo < (b + 1) * size * LANES and hi > b * size * LANES
            if len(shape) == 2 or not inside:
                if run:
                    vecs.append((run_at, jnp.concatenate(run).reshape(-1, LANES)))
                run = []
                if inside:
                    mats.append((lo // LANES, grads[i]))
            else:
                run_at = run_at if run else lo // LANES
                run.append(grads[i] if i < len(grads) else tail)
        if run:
            vecs.append((run_at, jnp.concatenate(run).reshape(-1, LANES)))

        def half(core):
            return flatten(pos, b, mats, vecs, plan, core)

        return Reduce(half)

    if fast:
        r3 = block_of(3)
        r3.stage()
        r2 = block_of(2)
        r2.stage()
    grads[11] = dot_l(h2, dqkv_s)
    sums = row_sum(dqkv_s)
    grads[12], grads[13] = sums[:d], sums[2 * d :]
    if fast:
        dx1, grads[11] = advance((r3, r2), dx1, grads[11])

    da_t = product_back(dx1, w_fc).astype(BF)
    do_t = product_back(da_t, w_out_t).astype(BF)
    grads[7], grads[8] = dot_l(a_t, dx1), row_sum(dx1)
    if fast:
        do_t, grads[7] = advance((r3, r2), do_t, grads[7])
        r1 = block_of(1)
        r1.stage()
    dqkv_t = attend_back(qkv_t, same, do_t.reshape(micro * clips, span_t, d), d).reshape(tokens, 3 * d)
    if fast:
        (dqkv_t,) = advance((r3, r2, r1), dqkv_t)
    sums = row_sum(dqkv_t)
    grads[3], grads[4] = sums[:d], sums[2 * d :]
    grads[5], grads[6] = dot_l(o_t, da_t), row_sum(da_t)
    grads[2] = dot_l(h1, dqkv_t)
    if fast:
        grads[2], dqkv_t = advance((r1,), grads[2], dqkv_t)
        grads[0] = grads[1] = jnp.zeros((d,), F32)
        r0 = block_of(0)
        r0.stage()
    dh1 = product_back(dqkv_t, w_qkv_t)
    back1, grad_tg, grad_tb = norm_back(hat1, scale1, tg, dh1)
    if fast:
        norm_sum = SumAll(jnp.concatenate([grad_tg, grad_tb]).reshape(-1, LANES))
        norm_sum.stage()
        back1, out = advance((r3, r2, r1, r0, norm_sum), back1, out)
        (back1,) = advance((r1, r0, norm_sum), back1)
    else:
        grads[0], grads[1] = grad_tg, grad_tb
    out = out.reshape(inputs.shape) * live_low
    input_grad = (dx1.astype(F32) + back1).astype(BF).reshape(inputs.shape)

    if fast:
        advance((r0, norm_sum))
        advance((r0,))
        first = (pos[0] + pos[1] + pos[2] == 0).astype(F32)
        extra = norm_sum.state[0] * first
        extra = jnp.pad(extra, ((0, plan.part - extra.shape[0]), (0, 0)))
        param_grad = return_quarters([r0.state + extra, r1.state, r2.state, r3.state], plan, pos)
    else:
        flat = jnp.concatenate([g.reshape(-1) for g in grads] + [jnp.zeros((full_length - used,), F32)])
        param_grad = lax.psum_scatter(flat, BOTH, scatter_dimension=0, tiled=True)
    return (out, input_grad, param_grad)


def solution(mesh):
    tokens = P(None, "dp", None, "sp", None)
    return jax.shard_map(
        layer,
        mesh=mesh,
        in_specs=(tokens, tokens, P(BOTH), P(None, "dp"), P(None, "dp", "sp")),
        out_specs=(tokens, tokens, P(BOTH)),
        check_vma=False,
    )
```
